32 devices in a mesh: ctx: 16 (over z, x, core), head: 2 (over y).
Axes of the slice: x: 2, y: 2, z: 4, core: 2. Of those that a mesh axis runs over, the one named last changes fastest.
Arguments:
- query_vectors: bfloat16 [2048, 5120], P('ctx', 'head'), may hold values from -128 to 128
- key_vectors: bfloat16 [2048, 5120], P('ctx', 'head'), may hold values from -128 to 128
- value_vectors: bfloat16 [2048, 5120], P('ctx', 'head'), may hold values from -24 to 24
- output_grad: bfloat16 [2048, 5120], P('ctx', 'head'), may hold values from -6 to 6
- query_gain: float32 [5120], P('head'), may hold values from 0.1 to 1.9
- key_gain: float32 [5120], P('head'), may hold values from 0.1 to 1.9
- block_pairs: int32 [16, 7, 2], P('ctx'), may hold values from 0 to 15, as said below
- pair_counts: int32 [16], P('ctx'), may hold values from 1 to 7, as said below
Outputs:
- attended: bfloat16 [2048, 5120], P('ctx', 'head')
- query_grad: bfloat16 [2048, 5120], P('ctx', 'head')
- key_grad: bfloat16 [2048, 5120], P('ctx', 'head')
- value_grad: bfloat16 [2048, 5120], P('ctx', 'head')
The draws below stay inside these ranges and needn't reach their ends.
Inputs may be any that keep to these rules, and one draw needn't show every extreme that they name: For span c the first pair_counts[c] slots of block_pairs[c] hold distinct pairs; the query block is c (a mask block is one 128-token span) and the key block is c - o, where o is 0 or plus or minus a power of two no larger than 4; the pair (c, c) is always present. Later slots are to be ignored. `pair_counts`: some span uses all 7 slots.
All inputs are finite; a program needn't handle non-finite values.
Results may differ from the reference program's by a relative error of at most 0.0085.
The reference program's roundings to bfloat16 on the way (of `query_norm`, `key_norm`, `weights` and `score_grad`) count: a program that leaves them out, or rounds other values in their place, can miss the bound.
Values may be sent and summed in bfloat16 or wider, within the bound.
No kernel may reach another device: no remote copies, remote signals or barrier semaphores. Data moves between devices by JAX's collectives and lax.ppermute only.
A program may use at most 128 MiB of HBM per device.

```python
import jax
import jax.numpy as jnp
from jax import lax

DIM = 5120
HEADS = 40
HEAD = 128
TOK_DEV = 128
SPANS = 16
TOKENS = 2048
QB = 1
NB = 16
LEVELS = 3
OFFSETS = 7
MAXP = 7


def offset_list_drawn(levels):
    result = [0]
    for height in range(levels):
        result = result + [2 ** height, -2 ** height]
    return result


def height_list(levels):
    result = [0]
    for height in range(levels):
        result = result + [height, height]
    return result


def mask_table(key):
    offsets = jnp.array(offset_list_drawn(LEVELS), jnp.int32)[None, None, :, None]
    heights = jnp.array(height_list(LEVELS), jnp.int32)[None, None, :, None]
    span_ids = jnp.arange(SPANS, dtype=jnp.int32)[:, None, None, None]
    local_query = jnp.arange(QB, dtype=jnp.int32)[None, :, None, None]
    local_key = jnp.arange(QB, dtype=jnp.int32)[None, None, None, :]
    other = span_ids - offsets
    inside = (other >= 0) & (other < SPANS)
    ceiling = jnp.broadcast_to(2 ** (heights + 1), (SPANS, QB, OFFSETS, QB))
    coins = jax.random.randint(jax.random.fold_in(key, 1), (SPANS, QB, OFFSETS, QB), 0, ceiling)
    chosen = jax.random.randint(jax.random.fold_in(key, 2), (), SPANS // 4, 3 * SPANS // 4)
    keep = inside & ((offsets == 0) | (coins == 0) | (span_ids == chosen))
    query_block = jnp.broadcast_to(span_ids * QB + local_query, keep.shape).reshape(SPANS, MAXP)
    key_block = jnp.broadcast_to((other * QB + local_key) % NB, keep.shape).reshape(SPANS, MAXP)
    keep_flat = keep.reshape(SPANS, MAXP).astype(jnp.int32)
    ranking = (1 - keep_flat) * MAXP + jnp.arange(MAXP, dtype=jnp.int32)[None, :]
    ordering = jnp.argsort(ranking, axis=1)
    pairs = jnp.stack([jnp.take_along_axis(query_block, ordering, axis=1), jnp.take_along_axis(key_block, ordering, axis=1)], axis=2)
    return (pairs.astype(jnp.int32), jnp.sum(keep_flat, axis=1).astype(jnp.int32))


def draw_block_pairs(key, part):
    return mask_table(key)[0]


def draw_pair_counts(key, part):
    return mask_table(key)[1]


def vector_table(key):
    col_ids = jnp.arange(DIM, dtype=jnp.int32)[None, :]
    base_query = jnp.clip(jax.random.normal(jax.random.fold_in(key, 11), (TOKENS, DIM), jnp.float32), -5.0, 5.0)
    base_key = jnp.clip(jax.random.normal(jax.random.fold_in(key, 12), (TOKENS, DIM), jnp.float32), -5.0, 5.0)
    col_draw = jax.random.uniform(jax.random.fold_in(key, 13), (1, DIM), jnp.float32)
    row_query = jax.random.uniform(jax.random.fold_in(key, 14), (TOKENS, 1), jnp.float32)
    row_key = jax.random.uniform(jax.random.fold_in(key, 15), (TOKENS, 1), jnp.float32)
    position = col_ids.astype(jnp.float32) / DIM
    col_scale = 10.0 ** (0.5 * col_draw + 0.5 * position - 0.5)
    query_scale = 10.0 ** (row_query - 0.5)
    key_scale = 10.0 ** (row_key - 0.5)
    queries = base_query * col_scale * query_scale
    key_rows = base_key * col_scale * key_scale
    return (queries, key_rows)


def draw_query_vectors(key, part):
    return vector_table(key)[0].astype(jnp.bfloat16)


def draw_key_vectors(key, part):
    return vector_table(key)[1].astype(jnp.bfloat16)


def steps_of(own_key, shape, cuts, least, largest):
    def one(dim, blocks):
        steps = jax.random.uniform(jax.random.fold_in(jax.random.fold_in(own_key, 6), dim), (blocks,), jnp.float32, least / len(cuts), largest / len(cuts))
        return jnp.repeat(jnp.exp(steps), shape[dim] // blocks).reshape((-1,) + (1,) * (len(shape) - dim - 1))

    loudness = one(*cuts[0])
    for cut in cuts[1:]:
        loudness = loudness * one(*cut)
    return loudness


def bell_draw(key, dims, deviation, reach, shards=(), held_as=jnp.bfloat16):
    factor_of = steps_of(key, dims, shards, -0.22, 0.18) if shards else 1.0
    values = jax.random.normal(key, dims, jnp.float32) * deviation * factor_of
    return jnp.minimum(jnp.maximum(values, -reach), reach).astype(held_as)


def setup_inputs(seed: int = 0) -> dict:
    key_of = jax.random.split(jax.random.key(seed), 9)
    query_vectors = draw_query_vectors(jax.random.fold_in(key_of[8], 71), 0)
    key_vectors = draw_key_vectors(jax.random.fold_in(key_of[8], 71), 0)
    value_vectors = bell_draw(key_of[2], (TOKENS, DIM), 4.0, 24.0, ((0, 16), (1, 2)))
    output_grad = bell_draw(key_of[3], (TOKENS, DIM), 1.0, 6.0, ((0, 16), (1, 2)))
    query_gain = jnp.clip(1.0 + 0.18 * jax.random.normal(key_of[4], (DIM,), jnp.float32), 0.1, 1.9)
    key_gain = jnp.clip(1.0 + 0.18 * jax.random.normal(key_of[5], (DIM,), jnp.float32), 0.1, 1.9)
    block_pairs = draw_block_pairs(jax.random.fold_in(key_of[8], 71), 0)
    pair_counts = draw_pair_counts(jax.random.fold_in(key_of[8], 71), 0)
    return dict(query_vectors=query_vectors, key_vectors=key_vectors, value_vectors=value_vectors, output_grad=output_grad, query_gain=query_gain, key_gain=key_gain, block_pairs=block_pairs, pair_counts=pair_counts)


epsilon = 1e-06
lowest = -1e+30

def offset_list(levels):
    result = [0]
    for height in range(levels):
        result = result + [2 ** height, -2 ** height]
    return result

def rms_forward(vectors, gain):
    floats = vectors.astype(jnp.float32)
    rstd_rows = lax.rsqrt(lax.optimization_barrier(jnp.mean(floats * floats, axis=1, keepdims=True)) + epsilon)
    unit_rows = floats * rstd_rows
    return (unit_rows, rstd_rows, (unit_rows * gain.astype(jnp.float32)[None, :]).astype(jnp.bfloat16))

def rms_backward(norm_grad, unit_rows, rstd_rows, gain):
    scaled = norm_grad * gain.astype(jnp.float32)[None, :]
    inner = lax.optimization_barrier(jnp.mean(scaled * unit_rows, axis=1, keepdims=True))
    return (rstd_rows * (scaled - unit_rows * inner)).astype(jnp.bfloat16)

def masked(values, tile_mask, filler):
    head_count = values.shape[0]
    qblocks = tile_mask.shape[0]
    kblocks = tile_mask.shape[1]
    shaped = values.reshape(head_count, qblocks, values.shape[1] // qblocks, kblocks, values.shape[2] // kblocks)
    return jnp.where(tile_mask[None, :, None, :, None], shaped, filler).reshape(values.shape)

def block_scores(queries, key_rows, tile_mask):
    scaling = HEAD ** (-0.5)
    products = jnp.einsum('qhd,khd->hqk', queries.astype(jnp.float32), key_rows.astype(jnp.float32)) * scaling
    return masked(products, tile_mask, lowest)

def tile_grads(queries, out_grads, logsum, row_delta, key_rows, value_rows, tile_mask):
    scaling = HEAD ** (-0.5)
    scores = block_scores(queries, key_rows, tile_mask)
    weights = jnp.exp(scores - logsum[:, :, None])
    weights_low = weights.astype(jnp.bfloat16)
    weight_grad = jnp.einsum('qhd,khd->hqk', out_grads.astype(jnp.float32), value_rows.astype(jnp.float32))
    score_grad = (scaling * weights * (weight_grad - row_delta[:, :, None])).astype(jnp.bfloat16)
    query_part = jnp.einsum('hqk,khd->qhd', score_grad.astype(jnp.float32), key_rows.astype(jnp.float32)).astype(jnp.bfloat16)
    key_part = jnp.einsum('hqk,qhd->khd', score_grad.astype(jnp.float32), queries.astype(jnp.float32)).astype(jnp.bfloat16)
    value_part = jnp.einsum('hqk,qhd->khd', weights_low.astype(jnp.float32), out_grads.astype(jnp.float32)).astype(jnp.bfloat16)
    return (query_part, key_part, value_part)

def reference(query_vectors, key_vectors, value_vectors, output_grad, query_gain, key_gain, block_pairs, pair_counts):
    shifts = offset_list(LEVELS)
    query_unit, query_rstd, query_norm = rms_forward(query_vectors, query_gain)
    key_unit, key_rstd, key_norm = rms_forward(key_vectors, key_gain)
    live_slots = jnp.arange(MAXP, dtype=jnp.int32)[None, :] < pair_counts[:, None]
    tile_table = jnp.zeros((NB, NB), jnp.int32).at[block_pairs[:, :, 0].reshape(-1), block_pairs[:, :, 1].reshape(-1)].max(live_slots.astype(jnp.int32).reshape(-1))
    query_spans = query_norm.reshape(SPANS, TOK_DEV, HEADS, HEAD)
    key_spans = key_norm.reshape(SPANS, TOK_DEV, HEADS, HEAD)
    value_spans = value_vectors.reshape(SPANS, TOK_DEV, HEADS, HEAD)
    grad_spans = output_grad.reshape(SPANS, TOK_DEV, HEADS, HEAD)

    def tile_at(span_index, offset):
        other = span_index - offset
        inside = (other >= 0) & (other < SPANS)
        clipped = jnp.clip(other, 0, SPANS - 1).astype(jnp.int32)
        tile_mask = lax.dynamic_slice(tile_table, (span_index * QB, clipped * QB), (QB, QB)) > 0
        return (tile_mask & inside, clipped)

    def forward_span(span_index):
        queries = query_spans[span_index]
        stats = (jnp.full((HEADS, TOK_DEV), lowest, jnp.float32), jnp.zeros((HEADS, TOK_DEV), jnp.float32))
        for offset in shifts:
            tile_mask, clipped = tile_at(span_index, offset)
            key_rows = key_spans[clipped]

            def update(carry, key_rows=key_rows, tile_mask=tile_mask):
                scores = block_scores(queries, key_rows, tile_mask)
                running_max = jnp.maximum(carry[0], lax.optimization_barrier(jnp.max(scores, axis=2)))
                running_sum = carry[1] * jnp.exp(carry[0] - running_max) + lax.optimization_barrier(jnp.sum(jnp.exp(scores - running_max[:, :, None]), axis=2))
                return (running_max, running_sum)
            stats = lax.cond(jnp.any(tile_mask), update, lambda carry: carry, stats)
        logsum = stats[0] + jnp.log(stats[1])
        totals = jnp.zeros((TOK_DEV, HEADS, HEAD), jnp.float32)
        for offset in shifts:
            tile_mask, clipped = tile_at(span_index, offset)
            key_rows = key_spans[clipped]
            value_rows = value_spans[clipped]

            def accumulate(current, key_rows=key_rows, value_rows=value_rows, tile_mask=tile_mask):
                scores = block_scores(queries, key_rows, tile_mask)
                weights = jnp.exp(scores - logsum[:, :, None]).astype(jnp.bfloat16)
                return current + jnp.einsum('hqk,khd->qhd', weights.astype(jnp.float32), value_rows.astype(jnp.float32))
            totals = lax.cond(jnp.any(tile_mask), accumulate, lambda current: current, totals)
        attended = totals.astype(jnp.bfloat16)
        row_delta = lax.optimization_barrier(jnp.sum(grad_spans[span_index].astype(jnp.float32) * attended.astype(jnp.float32), axis=2)).T
        return (attended, logsum, row_delta)
    attended, logsums, deltas = lax.map(forward_span, jnp.arange(SPANS, dtype=jnp.int32))

    def backward_step(carry, span_index):
        key_sum, value_sum = carry
        queries = query_spans[span_index]
        out_grads = grad_spans[span_index]
        query_total = jnp.zeros((TOK_DEV, HEADS, HEAD), jnp.float32)
        for offset in shifts:
            tile_mask, clipped = tile_at(span_index, offset)
            key_rows = key_spans[clipped]
            value_rows = value_spans[clipped]
            empty = jnp.zeros((TOK_DEV, HEADS, HEAD), jnp.bfloat16)
            parts = lax.cond(jnp.any(tile_mask), lambda: tile_grads(queries, out_grads, logsums[span_index], deltas[span_index], key_rows, value_rows, tile_mask), lambda: (empty, empty, empty))
            query_total = query_total + parts[0].astype(jnp.float32)
            key_sum = key_sum.at[clipped].add(parts[1].astype(jnp.float32))
            value_sum = value_sum.at[clipped].add(parts[2].astype(jnp.float32))
        return ((key_sum, value_sum), query_total)
    zero_sum = jnp.zeros((SPANS, TOK_DEV, HEADS, HEAD), jnp.float32)
    (key_sum, value_sum), query_total = lax.scan(backward_step, (zero_sum, zero_sum), jnp.arange(SPANS, dtype=jnp.int32))
    query_grad = rms_backward(query_total.reshape(TOKENS, DIM), query_unit, query_rstd, query_gain)
    key_grad = rms_backward(key_sum.reshape(TOKENS, DIM), key_unit, key_rstd, key_gain)
    value_grad = value_sum.astype(jnp.bfloat16).reshape(TOKENS, DIM)
    return (attended.reshape(TOKENS, DIM), query_grad, key_grad, value_grad)
```

```python
import functools

import jax
import jax.numpy as jnp
from jax import lax
from jax.experimental import pallas as pl
from jax.experimental.pallas import tpu as pltpu
from jax.sharding import Mesh
from jax.sharding import PartitionSpec as P

HEAD = 128
epsilon = 1e-06
lowest = -1e30
LOG2E = 1.4426950408889634
SCALE = HEAD ** (-0.5)
bf16 = jnp.bfloat16
f32 = jnp.float32


def offset_list(levels):
    result = [0]
    for height in range(levels):
        result = result + [2**height, -(2**height)]
    return result


def plan(spans, heads_here):
    levels = spans.bit_length() - 2
    reach = 2 ** (levels - 1)
    group = reach if heads_here % reach == 0 and spans % reach == 0 else 1
    offsets = sorted(offset_list(levels), reverse=True)
    if group > 1:
        distances = [-1, 0, 1]
    else:
        distances = sorted(-o for o in offsets)
    return group, offsets, distances


def dot(a, b, ca, cb):
    return lax.dot_general(a, b, (((ca,), (cb,)), ((), ())), preferred_element_type=f32)


def attend(place, *refs, group, offsets, distances):
    nd = len(distances)
    ng = group * nd
    noff = len(offsets)
    it = iter(refs)
    qd = [next(it) for _ in range(group)]
    kv = [[next(it) for _ in range(group)] for _ in range(nd)]
    rstd_ref, bias_ref, qgain_ref, kgain_ref = (next(it) for _ in range(4))
    out_o = [next(it) for _ in range(group)]
    out_q = [next(it) for _ in range(group)]
    out_kv = [next(it) for _ in range(nd)]
    inner_ref = next(it)
    keys, vals, dkeys, dvals, inners, rcols = (next(it) for _ in range(6))
    home = distances.index(0)
    head = pl.program_id(0)
    r = place[0]

    @pl.when(head == 0)
    def _():
        rcols[...] = jnp.transpose(rstd_ref[...])
        inners[...] = jnp.zeros_like(inners)

    qgain = qgain_ref[...]
    kgain = kgain_ref[...]

    def rows(slot):
        return pl.ds(pl.multiple_of(slot * HEAD, HEAD), HEAD)

    def column(i):
        return rcols[:, i : i + 1]

    for d in range(nd):
        for m in range(group):
            at = rows(d * group + (m ^ r))
            unit = kv[d][m][0].astype(f32) * column(group + d * group + m)
            keys[at, :] = (unit * kgain).astype(bf16)
            vals[at, :] = kv[d][m][1]
    dkeys[...] = jnp.zeros_like(dkeys)
    dvals[...] = jnp.zeros_like(dvals)

    for m in range(group):
        s = m ^ r
        unit = qd[m][0].astype(f32) * column(m)
        q = (unit * qgain).astype(bf16)
        g = qd[m][1]
        if group > 1:
            slots = [home * group + s - o for o in offsets]
        else:
            slots = [distances.index(-o) for o in offsets]
        k = jnp.concatenate([keys[rows(x), :] for x in slots], axis=0)
        v = jnp.concatenate([vals[rows(x), :] for x in slots], axis=0)
        scores = dot(q, k, 1, 1) * (SCALE * LOG2E) + bias_ref[m : m + 1, :]
        top = jnp.max(scores, axis=1, keepdims=True)
        e = jnp.exp2(scores - top)
        p = e * (1.0 / jnp.sum(e, axis=1, keepdims=True))
        p_low = p.astype(bf16)
        o = dot(p_low, v, 1, 0).astype(bf16)
        out_o[m][...] = o
        delta = jnp.sum(g.astype(f32) * o.astype(f32), axis=1, keepdims=True)
        dp = dot(g, v, 1, 1)
        ds = (p * SCALE * (dp - delta)).astype(bf16)
        dq = dot(ds, k, 1, 0)
        out_q[m][...] = dq
        inners[m] += dq * qgain * unit
        dk = dot(ds, q, 0, 0)
        dv = dot(p_low, g, 0, 0)
        for j in range(noff):
            dkeys[rows(slots[j]), :] += dk[j * HEAD : (j + 1) * HEAD]
            dvals[rows(slots[j]), :] += dv[j * HEAD : (j + 1) * HEAD]

    for d in range(nd):
        for m in range(group):
            at = rows(d * group + (m ^ r))
            unit = kv[d][m][0].astype(f32) * column(group + d * group + m)
            dk = dkeys[at, :]
            inners[group + d * group + m] += dk * kgain * unit
            out_kv[d][0, m] = dk.astype(out_kv[d].dtype)
            out_kv[d][1, m] = dvals[at, :].astype(out_kv[d].dtype)

    @pl.when(head == pl.num_programs(0) - 1)
    def _():
        lanes = lax.broadcasted_iota(jnp.int32, (HEAD, HEAD), 1)
        table = jnp.zeros((HEAD, HEAD), f32)
        for base in range(0, group + ng, group):
            for m in range(group):
                total = jnp.sum(inners[base + m], axis=1, keepdims=True)
                table = jnp.where(lanes == base + (m ^ r), total, table)
        inner_ref[...] = jnp.transpose(table)


def attention(place, qd, kv, rstd, bias, query_gain, key_gain, group, offsets, distances):
    width = qd[0].shape[2]
    heads = width // HEAD
    nd = len(distances)
    ng = nd * group
    noff = len(offsets)
    pair = pl.BlockSpec((2, HEAD, HEAD), lambda h, _: (0, 0, h))
    flat = pl.BlockSpec((HEAD, HEAD), lambda h, _: (0, h))
    table = pl.BlockSpec((HEAD, HEAD), lambda h, _: (0, 0))
    gain = pl.BlockSpec((1, HEAD), lambda h, _: (0, h))
    grads = pl.BlockSpec((2, group, HEAD, HEAD), lambda h, _: (0, 0, 0, h))
    home = distances.index(0)
    outs = (
        [jax.ShapeDtypeStruct((HEAD, width), bf16)] * group
        + [jax.ShapeDtypeStruct((HEAD, width), f32)] * group
        + [
            jax.ShapeDtypeStruct((2, group, HEAD, width), f32 if d == home else bf16)
            for d in range(nd)
        ]
        + [jax.ShapeDtypeStruct((HEAD, HEAD), f32)]
    )
    work = heads * group * noff * 6 * 2 * HEAD**3
    result = pl.pallas_call(
        functools.partial(attend, group=group, offsets=offsets, distances=distances),
        grid_spec=pltpu.PrefetchScalarGridSpec(
            num_scalar_prefetch=1,
            grid=(heads,),
            in_specs=[pair] * (group + ng)
            + [table, pl.BlockSpec((group, noff * HEAD), lambda h, _: (0, 0)), gain, gain],
            out_specs=[flat] * (2 * group) + [grads] * nd + [table],
            scratch_shapes=[
                pltpu.VMEM((ng * HEAD, HEAD), bf16),
                pltpu.VMEM((ng * HEAD, HEAD), bf16),
                pltpu.VMEM((ng * HEAD, HEAD), f32),
                pltpu.VMEM((ng * HEAD, HEAD), f32),
                pltpu.VMEM((group + ng, HEAD, HEAD), f32),
                pltpu.VMEM((HEAD, HEAD), f32),
            ],
        ),
        out_shape=outs,
        compiler_params=pltpu.CompilerParams(vmem_limit_bytes=40 * 2**20),
        cost_estimate=pl.CostEstimate(
            flops=work, bytes_accessed=12 * 2**20, transcendentals=work // 1536
        ),
        name="attend",
    )(
        place,
        *qd,
        *[piece for block in kv for piece in block],
        rstd,
        bias,
        query_gain,
        key_gain,
    )
    return (
        result[:group],
        result[group : 2 * group],
        result[2 * group : 2 * group + nd],
        result[2 * group + nd],
    )


def local(
    query_vectors,
    key_vectors,
    value_vectors,
    output_grad,
    query_gain,
    key_gain,
    block_pairs,
    pair_counts,
    *,
    group,
    offsets,
    distances,
    heads_all,
):
    row_count, col_count = query_vectors.shape
    width = col_count // group
    features = heads_all * HEAD
    blocks = lax.axis_size("block")
    block = lax.axis_index("block")
    r = lax.axis_index("place")
    span = block * group + r
    home = distances.index(0)

    def chunk(array, index):
        return lax.dynamic_slice_in_dim(array, index * width, width, axis=1)

    def swap(x, m):
        return lax.ppermute(x, "place", [(i, i ^ m) for i in range(group)]) if m else x

    def moved(x, by):
        return lax.ppermute(
            x, "block", [(i, i + by) for i in range(blocks) if 0 <= i + by < blocks]
        )

    def pieces(a, b):
        return [swap(jnp.stack([chunk(a, r ^ m), chunk(b, r ^ m)]), m) for m in range(group)]

    kv_home = pieces(key_vectors, value_vectors)
    kv = [
        [moved(x, -by) if by else x for x in kv_home]
        for by in distances
    ]
    qd = pieces(query_vectors, output_grad)

    query_float = query_vectors.astype(f32)
    key_float = key_vectors.astype(f32)
    live = jnp.arange(block_pairs.shape[1], dtype=jnp.int32) < pair_counts[0]
    steps = block_pairs[0, :, 0] - block_pairs[0, :, 1]
    wanted = jnp.array(offsets, jnp.int32)
    flags = jnp.any(live[:, None] & (steps[:, None] == wanted[None, :]), axis=0)
    flag_row = jnp.zeros((HEAD,), f32).at[: len(offsets)].set(flags.astype(f32))
    mine = jnp.stack(
        [jnp.sum(query_float * query_float, axis=1), jnp.sum(key_float * key_float, axis=1), flag_row]
    )
    slots = jnp.arange(group, dtype=jnp.int32)
    sums = lax.psum(
        jnp.where((slots == r)[:, None, None], mine[None], 0.0), ("place", "head")
    )
    sums = sums[slots ^ r]
    key_sums = jnp.concatenate([moved(sums[:, 1], -by) if by else sums[:, 1] for by in distances])
    rstd = lax.rsqrt(jnp.concatenate([sums[:, 0], key_sums]) / features + epsilon)
    bias = jnp.where(sums[:, 2, : len(offsets)] > 0.5, 0.0, lowest)
    bias = jnp.repeat(bias, HEAD, axis=1)
    own_gains = [chunk(x[None, :], r) for x in (query_gain, key_gain)]

    o_parts, q_parts, kv_parts, inner = attention(
        jnp.reshape(r, (1,)).astype(jnp.int32),
        qd,
        kv,
        jnp.pad(rstd, ((0, HEAD - rstd.shape[0]), (0, 0))),
        bias,
        *own_gains,
        group,
        offsets,
        distances,
    )

    def gathered(parts):
        stacked = jnp.stack([swap(x, m) for m, x in enumerate(parts)])
        return jnp.concatenate(
            [lax.dynamic_index_in_dim(stacked, j ^ r, 0, keepdims=False) for j in range(group)],
            axis=-1,
        )

    attended = gathered(o_parts)
    back = [moved(kv_parts[d], by) for d, by in enumerate(distances) if by]
    key_inner = inner[group + home * group : 2 * group + home * group]
    for d, by in enumerate(distances):
        if by:
            key_inner = key_inner + moved(inner[group + d * group : 2 * group + d * group], by)
    inners = lax.psum(jnp.stack([inner[:group], key_inner]), ("place", "head")) / features
    inners = inners[:, slots ^ r]

    def finished(raw, rstd_row, gain, grad, inner_row):
        unit = raw.astype(f32) * rstd_row[:, None]
        return (rstd_row[:, None] * (gain * grad - unit * inner_row[:, None])).astype(bf16)

    query_grad = gathered(
        [
            finished(qd[m][0], rstd[m], own_gains[0], q_parts[m], inners[0, m])
            for m in range(group)
        ]
    )
    both = []
    for m in range(group):
        total = kv_parts[home][:, m]
        for x in back:
            total = total + x[:, m].astype(f32)
        key_part = finished(
            kv_home[m][0], rstd[group + home * group + m], own_gains[1], total[0], inners[1, m]
        )
        both.append(jnp.stack([key_part, total[1].astype(bf16)]))
    both = gathered(both)
    return (attended, query_grad, both[0], both[1])


def solution(mesh):
    spans, head_groups = mesh.devices.shape
    heads_all = 5120 // HEAD
    group, offsets, distances = plan(spans, heads_all // head_groups)
    inner_mesh = Mesh(
        mesh.devices.reshape(spans // group, group, head_groups), ("block", "place", "head")
    )
    ctx = ("block", "place")
    placed = (
        P(ctx, "head"),
        P(ctx, "head"),
        P(ctx, "head"),
        P(ctx, "head"),
        P("head"),
        P("head"),
        P(ctx, None, None),
        P(ctx),
    )
    return jax.shard_map(
        functools.partial(
            local, group=group, offsets=offsets, distances=distances, heads_all=heads_all
        ),
        mesh=inner_mesh,
        in_specs=placed,
        out_specs=(P(ctx, "head"),) * 4,
        check_vma=False,
    )
```

```python
import functools

import jax
import jax.numpy as jnp
import numpy as np
from jax import lax
from jax.experimental import pallas as pl
from jax.experimental.pallas import tpu as pltpu
from jax.sharding import Mesh
from jax.sharding import PartitionSpec as P

DIM = 5120
HEAD = 128
TAIL = 16
epsilon = 1e-06
lowest = -1e30
LOG2E = 1.4426950408889634
SCALE = HEAD ** (-0.5)
bf16 = jnp.bfloat16
f32 = jnp.float32
WIDE = pltpu.CompilerParams(vmem_limit_bytes=60 * 2**20)


def offset_list(levels):
    result = [0]
    for height in range(levels):
        result = result + [2**height, -(2**height)]
    return result


class Plan:
    def __init__(self, spans, heads_here):
        levels = spans.bit_length() - 2
        reach = 2 ** (levels - 1)
        whole = heads_here % reach == 0 and spans % reach == 0
        self.group = reach if whole else 1
        self.offsets = sorted(offset_list(levels), reverse=True)
        self.distances = [-1, 0, 1] if self.group > 1 else sorted(self.offsets)
        self.home = self.distances.index(0)
        self.heads = heads_here // self.group
        self.chunks = CHUNKS(self.heads)
        if self.group > 1:
            self.slots = [[self.group + s - o for o in self.offsets] for s in range(self.group)]
        else:
            self.slots = [[self.distances.index(-o) for o in self.offsets]]


def CHUNKS(heads):
    return [(0, heads)]


def dot(a, b, ca, cb):
    return lax.dot_general(a, b, (((ca,), (cb,)), ((), ())), preferred_element_type=f32)


def attend(place, *refs, plan):
    group, nd, noff = plan.group, len(plan.distances), len(plan.offsets)
    it = iter(refs)
    qd = [next(it) for _ in range(group)]
    kv = [[next(it) for _ in range(group)] for _ in range(nd)]
    out_oq = [next(it) for _ in range(group)]
    out_kv = [next(it) for _ in range(nd)]
    keys, vals, queries, grads, weights, scored, outs, dqs, allow = (next(it) for _ in range(9))
    r = place[0]

    def rows(slot):
        if isinstance(slot, int):
            return pl.ds(slot * HEAD, HEAD)
        return pl.ds(pl.multiple_of(slot * HEAD, HEAD), HEAD)

    for m in range(group):
        at = rows(m ^ r)
        queries[at, :] = qd[m][0:HEAD]
        grads[at, :] = qd[m][HEAD : 2 * HEAD]
        allow[m ^ r] = qd[m][2 * HEAD : 2 * HEAD + TAIL].astype(f32)
        for d in range(nd):
            at = rows(d * group + (m ^ r))
            keys[at, :] = kv[d][m][0]
            vals[at, :] = kv[d][m][1]

    for s in range(group):
        q = queries[rows(s), :]
        g = grads[rows(s), :]
        k = jnp.concatenate([keys[rows(x), :] for x in plan.slots[s]], axis=0)
        v = jnp.concatenate([vals[rows(x), :] for x in plan.slots[s]], axis=0)
        bias = jnp.concatenate([allow[s, j : j + 1, :] for j in range(noff)], axis=1)
        scores = dot(q, k, 1, 1) * (SCALE * LOG2E) + bias
        top = jnp.max(scores, axis=1, keepdims=True)
        e = jnp.exp2(scores - top)
        p = e * (1.0 / jnp.sum(e, axis=1, keepdims=True))
        p_low = p.astype(bf16)
        o = dot(p_low, v, 1, 0).astype(bf16)
        delta = jnp.sum(g.astype(f32) * o.astype(f32), axis=1, keepdims=True)
        ds = (p * SCALE * (dot(g, v, 1, 1) - delta)).astype(bf16)
        weights[rows(s), :] = p_low
        scored[rows(s), :] = ds
        outs[rows(s), :] = o
        dqs[rows(s), :] = dot(ds, k, 1, 0).astype(bf16)

    for m in range(group):
        out_oq[m][0] = outs[rows(m ^ r), :]
        out_oq[m][1] = dqs[rows(m ^ r), :]

    for d in range(nd):
        for s in range(group):
            users = [
                (t, j)
                for t in range(group)
                for j in range(noff)
                if plan.slots[t][j] == d * group + s
            ]

            def stacked(ref):
                return jnp.concatenate([ref[rows(t), rows(j)] for t, j in users], axis=0)

            q = jnp.concatenate([queries[rows(t), :] for t, _ in users], axis=0)
            g = jnp.concatenate([grads[rows(t), :] for t, _ in users], axis=0)
            out_kv[d][s ^ r, 1] = dot(stacked(scored), q, 0, 0).astype(out_kv[d].dtype)
            out_kv[d][s ^ r, 0] = dot(stacked(weights), g, 0, 0).astype(out_kv[d].dtype)


def attention(place, qd, kv, plan):
    width = qd[0].shape[1]
    heads = width // HEAD
    group, nd, noff = plan.group, len(plan.distances), len(plan.offsets)
    ng = nd * group
    query = pl.BlockSpec((2 * HEAD + TAIL, HEAD), lambda h, _: (0, h))
    pair = pl.BlockSpec((2, HEAD, HEAD), lambda h, _: (0, 0, h))
    grads = pl.BlockSpec((group, 2, HEAD, HEAD), lambda h, _: (0, 0, 0, h))
    outs = [jax.ShapeDtypeStruct((2, HEAD, width), bf16)] * group + [
        jax.ShapeDtypeStruct((group, 2, HEAD, width), f32 if by == 0 else bf16)
        for by in plan.distances
    ]
    work = heads * group * noff * 6 * 2 * HEAD**3
    result = pl.pallas_call(
        functools.partial(attend, plan=plan),
        grid_spec=pltpu.PrefetchScalarGridSpec(
            num_scalar_prefetch=1,
            grid=(heads,),
            in_specs=[query] * group + [pair] * ng,
            out_specs=[pair] * group + [grads] * nd,
            scratch_shapes=[pltpu.VMEM((ng * HEAD, HEAD), bf16)] * 2
            + [pltpu.VMEM((group * HEAD, HEAD), bf16)] * 2
            + [pltpu.VMEM((group * HEAD, noff * HEAD), bf16)] * 2
            + [pltpu.VMEM((group * HEAD, HEAD), bf16)] * 2
            + [pltpu.VMEM((group, TAIL, HEAD), f32)],
        ),
        out_shape=outs,
        compiler_params=WIDE,
        cost_estimate=pl.CostEstimate(
            flops=work, bytes_accessed=2 * heads * 2**20, transcendentals=work // 1536
        ),
        name="attend",
    )(place, *qd, *[piece for block in kv for piece in block])
    return result[:group], result[group:]


def split(place, a_ref, b_ref, rstd_ref, gain_ref, *refs, plan, allowed):
    r = place[0]
    width = plan.heads * HEAD
    outs = iter(refs[allowed:])
    for first, count in plan.chunks:
        for m in range(plan.group):
            at = pl.ds(pl.multiple_of((m ^ r) * width + first * HEAD, HEAD), count * HEAD)
            a = (a_ref[:, at].astype(f32) * rstd_ref[:, 0:1] * gain_ref[:, at]).astype(bf16)
            out = next(outs)
            if allowed:
                out[0:HEAD, :] = a
                out[HEAD : 2 * HEAD, :] = b_ref[:, at]
                for h in range(count):
                    out[2 * HEAD : 2 * HEAD + TAIL, h * HEAD : (h + 1) * HEAD] = refs[0][...]
            else:
                out[0] = a
                out[1] = b_ref[:, at]


def pieces_of(place, a, b, rstd, gain, allow, plan):
    shapes = [
        jax.ShapeDtypeStruct(
            (2, HEAD, count * HEAD) if allow is None else (2 * HEAD + TAIL, count * HEAD), bf16
        )
        for _, count in plan.chunks
        for _ in range(plan.group)
    ]
    args = [a, b, rstd, gain] + ([] if allow is None else [allow])
    whole = pl.BlockSpec(memory_space=pltpu.VMEM)
    result = pl.pallas_call(
        functools.partial(split, plan=plan, allowed=allow is not None),
        grid_spec=pltpu.PrefetchScalarGridSpec(
            num_scalar_prefetch=1,
            grid=(),
            in_specs=[whole] * len(args),
            out_specs=[whole] * len(shapes),
        ),
        out_shape=shapes,
        compiler_params=pltpu.CompilerParams(vmem_limit_bytes=24 * 2**20),
        name="split",
    )(place, *args)
    return [
        result[c * plan.group : (c + 1) * plan.group] for c in range(len(plan.chunks))
    ]


def join(place, *refs, plan):
    group = plan.group
    count = len(plan.chunks) * group
    parts = refs[:count]
    raw_ref, rstd_ref, gain_ref, plain, normed, inner = refs[count:]
    r = place[0]
    width = plan.heads * HEAD
    total = jnp.zeros((HEAD, HEAD), f32)
    for c, (first, heads) in enumerate(plan.chunks):
        for m in range(group):
            base = (m ^ r) * width + first * HEAD
            part = parts[c * group + m]
            for h in range(heads):
                at = pl.ds(pl.multiple_of(base + h * HEAD, HEAD), HEAD)
                here = slice(h * HEAD, (h + 1) * HEAD)
                plain[:, at] = part[0, :, here]
                low = part[1, :, here]
                normed[:, at] = low
                total += low.astype(f32) * gain_ref[:, at] * raw_ref[:, at].astype(f32)
    inner[...] = jnp.broadcast_to(
        jnp.sum(total, axis=1, keepdims=True) * rstd_ref[:, 0:1], (HEAD, HEAD)
    )


def joined(place, parts, raw, rstd, gain, plan):
    shape = raw.shape
    flat = [x for chunk in parts for x in chunk]
    whole = pl.BlockSpec(memory_space=pltpu.VMEM)
    return pl.pallas_call(
        functools.partial(join, plan=plan),
        grid_spec=pltpu.PrefetchScalarGridSpec(
            num_scalar_prefetch=1,
            grid=(),
            in_specs=[whole] * (len(flat) + 3),
            out_specs=[whole] * 3,
        ),
        out_shape=[
            jax.ShapeDtypeStruct(shape, bf16),
            jax.ShapeDtypeStruct(shape, bf16),
            jax.ShapeDtypeStruct((HEAD, HEAD), f32),
        ],
        compiler_params=pltpu.CompilerParams(vmem_limit_bytes=24 * 2**20),
        name="join",
    )(place, *flat, raw, rstd, gain)


def local(
    query_vectors,
    key_vectors,
    value_vectors,
    output_grad,
    query_gain,
    key_gain,
    block_pairs,
    pair_counts,
    *,
    plan,
):
    row_count, col_count = query_vectors.shape
    group, offsets, distances = plan.group, plan.offsets, plan.distances
    features = col_count * lax.axis_size("head")
    blocks = lax.axis_size("block")
    r = lax.axis_index("place")
    place = jnp.reshape(r, (1,)).astype(jnp.int32)

    def swap(x, m):
        return lax.ppermute(x, "place", [(i, i ^ m) for i in range(group)]) if m else x

    def moved(x, by):
        if by == 0:
            return x
        return lax.ppermute(
            x, "block", [(i, i + by) for i in range(blocks) if 0 <= i + by < blocks]
        )

    def summed(x):
        step, count = 1, lax.axis_size("head")
        while step < count:
            x = x + lax.ppermute(x, "head", [(i, i ^ step) for i in range(count)])
            step *= 2
        return x

    query_float = query_vectors.astype(f32)
    key_float = key_vectors.astype(f32)
    squares = summed(
        jnp.stack(
            [jnp.sum(key_float * key_float, axis=1), jnp.sum(query_float * query_float, axis=1)]
        )
    )
    rstd = jnp.broadcast_to(
        lax.rsqrt(squares / features + epsilon)[:, :, None], (2, row_count, HEAD)
    )
    query_gain = query_gain[None, :]
    key_gain = key_gain[None, :]

    kv_home = pieces_of(place, key_vectors, value_vectors, rstd[0], key_gain, None, plan)
    kv_all = []
    for pieces in kv_home:
        mine = [swap(x, m) for m, x in enumerate(pieces)]
        kv_all.append([[moved(x, -by) for x in mine] for by in distances])

    live = jnp.arange(block_pairs.shape[1], dtype=jnp.int32) < pair_counts[0]
    steps = block_pairs[0, :, 0] - block_pairs[0, :, 1]
    wanted = jnp.array(offsets, jnp.int32)
    flags = jnp.any(live[:, None] & (steps[:, None] == wanted[None, :]), axis=0)
    bias = jnp.pad(jnp.where(flags, 0.0, lowest), (0, TAIL - len(offsets)))
    allow = jnp.broadcast_to(bias[:, None], (TAIL, HEAD)).astype(bf16)

    query_late, grad_late, *_ = lax.optimization_barrier(
        (query_vectors, output_grad, *[block[0] for block in kv_all[0]])
    )
    qd_home = pieces_of(place, query_late, grad_late, rstd[1], query_gain, allow, plan)

    oq_back, kv_back = [], []
    for c in range(len(plan.chunks)):
        qd = [swap(x, m) for m, x in enumerate(qd_home[c])]
        oq_parts, kv_parts = attention(place, qd, kv_all[c], plan)
        oq_back.append([swap(x, m) for m, x in enumerate(oq_parts)])
        back = [moved(kv_parts[d], by) for d, by in enumerate(distances) if by]
        total = []
        for m in range(group):
            x = kv_parts[plan.home][m]
            for y in back:
                x = x + y[m].astype(f32)
            total.append(swap(x.astype(bf16), m))
        kv_back.append(total)

    attended, query_norm_grad, query_inner = joined(
        place, oq_back, query_vectors, rstd[1], query_gain, plan
    )
    value_grad, key_norm_grad, key_inner = joined(
        place, kv_back, key_vectors, rstd[0], key_gain, plan
    )

    def finished(raw, rstd_wide, gain, grad, inner):
        inner = summed(inner[:, 0])[:, None] / features
        rstd_col = rstd_wide[:, 0:1]
        unit = raw.astype(f32) * rstd_col
        return (rstd_col * (gain * grad.astype(f32) - unit * inner)).astype(bf16)

    query_grad = finished(query_vectors, rstd[1], query_gain, query_norm_grad, query_inner)
    key_grad = finished(key_vectors, rstd[0], key_gain, key_norm_grad, key_inner)
    return (attended, query_grad, key_grad, value_grad)


def solution(mesh):
    spans, head_groups = mesh.devices.shape
    plan = Plan(spans, DIM // HEAD // head_groups)
    blocks = Mesh(
        mesh.devices.reshape(spans // plan.group, plan.group, head_groups),
        ("block", "place", "head"),
    )
    ctx = ("block", "place")
    placed = (
        P(ctx, "head"),
        P(ctx, "head"),
        P(ctx, "head"),
        P(ctx, "head"),
        P("head"),
        P("head"),
        P(ctx, None, None),
        P(ctx),
    )
    return jax.shard_map(
        functools.partial(local, plan=plan),
        mesh=blocks,
        in_specs=placed,
        out_specs=(P(ctx, "head"),) * 4,
        check_vma=False,
    )
```

```python
import functools

import jax
import jax.numpy as jnp
import numpy as np
from jax import lax
from jax.experimental import pallas as pl
from jax.experimental.pallas import tpu as pltpu
from jax.sharding import Mesh
from jax.sharding import PartitionSpec as P

DIM = 5120
HEAD = 128
TAIL = 16
epsilon = 1e-06
lowest = -1e30
LOG2E = 1.4426950408889634
SCALE = HEAD ** (-0.5)
bf16 = jnp.bfloat16
f32 = jnp.float32
WIDE = pltpu.CompilerParams(vmem_limit_bytes=60 * 2**20)


def offset_list(levels):
    result = [0]
    for height in range(levels):
        result = result + [2**height, -(2**height)]
    return result


class Plan:
    def __init__(self, spans, heads_here):
        levels = spans.bit_length() - 2
        reach = 2 ** (levels - 1)
        whole = reach == 4 and heads_here % reach == 0 and spans % reach == 0
        self.group = reach if whole else 1
        self.offsets = sorted(offset_list(levels), reverse=True)
        self.distances = [-1, 0, 1] if self.group > 1 else sorted(self.offsets)
        self.home = self.distances.index(0)
        self.heads = heads_here // self.group
        self.chunks = chunks_of(self.heads)
        self.pack = min(self.group, 2)
        if self.group > 1:
            self.slots = [[self.group + s - o for o in self.offsets] for s in range(self.group)]
        else:
            self.slots = [[self.distances.index(-o) for o in self.offsets]]


def chunks_of(heads):
    return [(0, heads)]


def busy(us):
    return pl.CostEstimate(flops=int(us * 1.1e9), bytes_accessed=int(us * 3.5e6), transcendentals=0)


def dot(a, b, ca, cb):
    return lax.dot_general(a, b, (((ca,), (cb,)), ((), ())), preferred_element_type=f32)


def attend(place, *refs, plan, first, heads):
    group, nd, noff = plan.group, len(plan.distances), len(plan.offsets)
    it = iter(refs)
    packs = group // plan.pack

    def unpacked():
        return [ref.at[i] for ref in [next(it) for _ in range(packs)] for i in range(plan.pack)]

    qd = [next(it) for _ in range(group)]
    kv = [unpacked() for _ in range(nd)]
    out_oq = [next(it) for _ in range(group)]
    out_kv = [next(it) for _ in range(nd)]
    keys, vals, queries, grads, weights, scored, outs, dqs, allow = (next(it) for _ in range(9))
    r = place[0]

    def rows(slot):
        if isinstance(slot, int):
            return pl.ds(slot * HEAD, HEAD)
        return pl.ds(pl.multiple_of(slot * HEAD, HEAD), HEAD)

    def one_head(h, _):
        source = pl.ds(pl.multiple_of((first + h) * HEAD, HEAD), HEAD)
        target = pl.ds(pl.multiple_of(h * HEAD, HEAD), HEAD)
        for m in range(group):
            at = rows(m ^ r)
            queries[at, :] = qd[m][0:HEAD, source]
            grads[at, :] = qd[m][HEAD : 2 * HEAD, source]
            allow[m ^ r] = qd[m][2 * HEAD : 2 * HEAD + TAIL, source].astype(f32)
            for d in range(nd):
                at = rows(d * group + (m ^ r))
                keys[at, :] = kv[d][m][0, :, source]
                vals[at, :] = kv[d][m][1, :, source]

        def rows_of(j):
            return slice(j * HEAD, (j + 1) * HEAD)

        spans = range(group)
        q = [queries[rows(s), :] for s in spans]
        g = [grads[rows(s), :] for s in spans]
        k = [jnp.concatenate([keys[rows(x), :] for x in plan.slots[s]], axis=0) for s in spans]
        v = [jnp.concatenate([vals[rows(x), :] for x in plan.slots[s]], axis=0) for s in spans]
        raw = [dot(q[s], k[s], 1, 1) for s in spans]
        dp = [dot(g[s], v[s], 1, 1) for s in spans]
        p = []
        for s in spans:
            bias = jnp.concatenate([allow[s, j : j + 1, :] for j in range(noff)], axis=1)
            scores = raw[s] * (SCALE * LOG2E) + bias
            e = jnp.exp2(scores - jnp.max(scores, axis=1, keepdims=True))
            p.append(e * (1.0 / jnp.sum(e, axis=1, keepdims=True)))
        low = [x.astype(bf16) for x in p]
        o = [dot(low[s], v[s], 1, 0).astype(bf16) for s in spans]
        ds = []
        for s in spans:
            delta = jnp.sum(g[s].astype(f32) * o[s].astype(f32), axis=1, keepdims=True)
            ds.append((p[s] * SCALE * (dp[s] - delta)).astype(bf16))
        for s in spans:
            outs[rows(s), :] = o[s]
            dqs[rows(s), :] = dot(ds[s], k[s], 1, 0).astype(bf16)

        for m in range(group):
            out_oq[m][0, :, target] = outs[rows(m ^ r), :]
            out_oq[m][1, :, target] = dqs[rows(m ^ r), :]

        for d in range(nd):
            for s in range(group):
                users = [
                    (t, j)
                    for t in range(group)
                    for j in range(noff)
                    if plan.slots[t][j] == d * group + s
                ]

                def stacked(values):
                    return jnp.concatenate([values[t][:, rows_of(j)] for t, j in users], axis=0)

                qs = jnp.concatenate([q[t] for t, _ in users], axis=0)
                gs = jnp.concatenate([g[t] for t, _ in users], axis=0)
                out_kv[d][s ^ r, 1, :, target] = dot(stacked(ds), qs, 0, 0).astype(out_kv[d].dtype)
                out_kv[d][s ^ r, 0, :, target] = dot(stacked(low), gs, 0, 0).astype(out_kv[d].dtype)
        return 0

    lax.fori_loop(0, heads, one_head, 0)


def attention(place, qd, kv, plan, first, heads):
    width = heads * HEAD
    group, nd, noff = plan.group, len(plan.distances), len(plan.offsets)
    ng = nd * group
    packs = group // plan.pack
    query = pl.BlockSpec((2 * HEAD + TAIL, HEAD), lambda h, _: (0, h + first))
    keyed = pl.BlockSpec((plan.pack, 2, HEAD, HEAD), lambda h, _: (0, 0, 0, h + first))
    packs = group // plan.pack
    whole = pl.BlockSpec(memory_space=pltpu.VMEM)
    outs = [jax.ShapeDtypeStruct((2, HEAD, width), bf16)] * group + [
        jax.ShapeDtypeStruct((group, 2, HEAD, width), f32 if by == 0 else bf16)
        for by in plan.distances
    ]
    result = pl.pallas_call(
        functools.partial(attend, plan=plan, first=first, heads=heads),
        grid_spec=pltpu.PrefetchScalarGridSpec(
            num_scalar_prefetch=1,
            grid=(),
            in_specs=[whole] * (group + nd * packs),
            out_specs=[whole] * (group + nd),
            scratch_shapes=[pltpu.VMEM((ng * HEAD, HEAD), bf16)] * 2
            + [pltpu.VMEM((group * HEAD, HEAD), bf16)] * 2
            + [pltpu.VMEM((group * HEAD, noff * HEAD), bf16)] * 2
            + [pltpu.VMEM((group * HEAD, HEAD), bf16)] * 2
            + [pltpu.VMEM((group, TAIL, HEAD), f32)],
        ),
        out_shape=outs,
        compiler_params=pltpu.CompilerParams(vmem_limit_bytes=36 * 2**20),
        cost_estimate=busy(4 * heads),
        name="attend",
    )(place, *qd, *[pack for block in kv for pack in block])
    return result[:group], result[group:]


def join(place, *refs, plan):
    group = plan.group
    count = len(plan.chunks) * group
    parts = refs[:count]
    raw_ref, rstd_ref, gain_ref, plain, normed, inner = refs[count:]
    r = place[0]
    column = jnp.transpose(jnp.broadcast_to(rstd_ref[...], (HEAD, HEAD)))[:, 0:1]
    width = plan.heads * HEAD
    total = jnp.zeros((HEAD, HEAD), f32)
    for c, (first, heads) in enumerate(plan.chunks):
        for m in range(group):
            base = (m ^ r) * width + first * HEAD
            part = parts[c * group + m]
            for h in range(heads):
                at = pl.ds(pl.multiple_of(base + h * HEAD, HEAD), HEAD)
                here = slice(h * HEAD, (h + 1) * HEAD)
                plain[:, at] = part[0, :, here]
                low = part[1, :, here]
                normed[:, at] = low
                total += low.astype(f32) * gain_ref[:, at] * raw_ref[:, at].astype(f32)
    inner[...] = jnp.broadcast_to(
        jnp.sum(total, axis=1, keepdims=True) * column, (HEAD, HEAD)
    )


def joined(place, parts, raw, rstd, gain, plan):
    shape = raw.shape
    flat = [x for chunk in parts for x in chunk]
    whole = pl.BlockSpec(memory_space=pltpu.VMEM)
    return pl.pallas_call(
        functools.partial(join, plan=plan),
        grid_spec=pltpu.PrefetchScalarGridSpec(
            num_scalar_prefetch=1,
            grid=(),
            in_specs=[whole] * (len(flat) + 3),
            out_specs=[whole] * 3,
        ),
        out_shape=[
            jax.ShapeDtypeStruct(shape, bf16),
            jax.ShapeDtypeStruct(shape, bf16),
            jax.ShapeDtypeStruct((HEAD, HEAD), f32),
        ],
        compiler_params=pltpu.CompilerParams(vmem_limit_bytes=24 * 2**20),
        cost_estimate=busy(2),
        name="join",
    )(place, *flat, raw, rstd, gain)


def local(
    query_vectors,
    key_vectors,
    value_vectors,
    output_grad,
    query_gain,
    key_gain,
    block_pairs,
    pair_counts,
    *,
    plan,
):
    row_count, col_count = query_vectors.shape
    group, offsets, distances = plan.group, plan.offsets, plan.distances
    features = col_count * lax.axis_size("head")
    width = col_count // group
    blocks = lax.axis_size("block")
    r = lax.axis_index("place")
    place = jnp.reshape(r, (1,)).astype(jnp.int32)

    def swap(x, m):
        return lax.ppermute(x, "place", [(i, i ^ m) for i in range(group)]) if m else x

    def moved(x, by):
        if by == 0:
            return x
        return lax.ppermute(
            x, "block", [(i, i + by) for i in range(blocks) if 0 <= i + by < blocks]
        )

    def summed(x):
        step, count = 1, lax.axis_size("head")
        while step < count:
            x = x + lax.ppermute(x, "head", [(i, i ^ step) for i in range(count)])
            step *= 2
        return x

    query_gain = query_gain[None, :]
    key_gain = key_gain[None, :]

    def chunk(x, m):
        return lax.dynamic_slice_in_dim(x, (r ^ m) * width, width, axis=1)

    squares = summed(
        jnp.stack([jnp.sum(jnp.square(x.astype(f32)), axis=1) for x in (key_vectors, query_vectors)])
    )
    my_rstd = lax.rsqrt(squares / features + epsilon)

    def normed(x, rstd, gain):
        return (x.astype(f32) * rstd[:, None] * gain).astype(bf16)

    key_norm = normed(key_vectors, my_rstd[0], key_gain)
    kv = [jnp.stack([chunk(key_norm, m), chunk(value_vectors, m)]) for m in range(group)]
    query_norm = normed(query_vectors, my_rstd[1], query_gain)
    live = jnp.arange(block_pairs.shape[1], dtype=jnp.int32) < pair_counts[0]
    steps = block_pairs[0, :, 0] - block_pairs[0, :, 1]
    wanted = jnp.array(offsets, jnp.int32)
    flags = jnp.any(live[:, None] & (steps[:, None] == wanted[None, :]), axis=0)
    bias = jnp.pad(jnp.where(flags, 0.0, lowest), (0, TAIL - len(offsets)))
    allow = jnp.broadcast_to(bias[:, None], (TAIL, width)).astype(bf16)
    qd = [
        jnp.concatenate([chunk(query_norm, m), chunk(output_grad, m), allow]) for m in range(group)
    ]

    kv = [swap(x, m) for m, x in enumerate(kv)]
    near = jnp.stack(kv[: plan.pack])
    near = [moved(near, -by) for by in distances]
    kv, qd = lax.optimization_barrier((kv, qd))
    qd = [swap(x, m) for m, x in enumerate(qd)]
    packs = [jnp.stack(kv[i : i + plan.pack]) for i in range(plan.pack, group, plan.pack)]
    packs, near, qd[group // 2 % group] = lax.optimization_barrier((packs, near, qd[group // 2 % group]))
    kv = [[x] + [moved(y, -by) for y in packs] for x, by in zip(near, distances)]

    oq_back, kv_back = [], []
    for first, count in plan.chunks:
        oq_parts, kv_parts = attention(place, qd, kv, plan, first, count)
        oq_back.append([swap(x, m) for m, x in enumerate(oq_parts)])
        back = [moved(kv_parts[d], by) for d, by in enumerate(distances) if by]
        total = []
        for m in range(group):
            x = kv_parts[plan.home][m]
            for y in back:
                x = x + y[m].astype(f32)
            total.append(swap(x.astype(bf16), m))
        kv_back.append(total)

    attended, query_norm_grad, query_inner = joined(
        place, oq_back, query_vectors, my_rstd[1:2], query_gain, plan
    )
    value_grad, key_norm_grad, key_inner = joined(
        place, kv_back, key_vectors, my_rstd[0:1], key_gain, plan
    )

    def finished(raw, rstd, gain, grad, inner):
        inner = summed(inner[:, 0])[:, None] / features
        rstd_col = rstd[0][:, None]
        unit = raw.astype(f32) * rstd_col
        return (rstd_col * (gain * grad.astype(f32) - unit * inner)).astype(bf16)

    query_grad = finished(query_vectors, my_rstd[1:2], query_gain, query_norm_grad, query_inner)
    key_grad = finished(key_vectors, my_rstd[0:1], key_gain, key_norm_grad, key_inner)
    return (attended, query_grad, key_grad, value_grad)


def solution(mesh):
    spans, head_groups = mesh.devices.shape
    plan = Plan(spans, DIM // HEAD // head_groups)
    blocks = Mesh(
        mesh.devices.reshape(spans // plan.group, plan.group, head_groups),
        ("block", "place", "head"),
    )
    ctx = ("block", "place")
    placed = (
        P(ctx, "head"),
        P(ctx, "head"),
        P(ctx, "head"),
        P(ctx, "head"),
        P("head"),
        P("head"),
        P(ctx, None, None),
        P(ctx),
    )
    return jax.shard_map(
        functools.partial(local, plan=plan),
        mesh=blocks,
        in_specs=placed,
        out_specs=(P(ctx, "head"),) * 4,
        check_vma=False,
    )
```

```python
import functools

import jax
import jax.numpy as jnp
import numpy as np
from jax import lax
from jax.experimental import pallas as pl
from jax.experimental.pallas import tpu as pltpu
from jax.sharding import Mesh
from jax.sharding import PartitionSpec as P

DIM = 5120
HEAD = 128
TAIL = 16
epsilon = 1e-06
lowest = -1e30
LOG2E = 1.4426950408889634
SCALE = HEAD ** (-0.5)
bf16 = jnp.bfloat16
f32 = jnp.float32
WIDE = pltpu.CompilerParams(vmem_limit_bytes=60 * 2**20)


def offset_list(levels):
    result = [0]
    for height in range(levels):
        result = result + [2**height, -(2**height)]
    return result


class Plan:
    def __init__(self, spans, heads_here):
        levels = spans.bit_length() - 2
        reach = 2 ** (levels - 1)
        whole = reach == 4 and heads_here % reach == 0 and spans % reach == 0
        self.group = reach if whole else 1
        self.offsets = sorted(offset_list(levels), reverse=True)
        self.distances = [-1, 0, 1] if self.group > 1 else sorted(self.offsets)
        self.home = self.distances.index(0)
        self.heads = heads_here // self.group
        self.chunks = chunks_of(self.heads)
        self.pack = min(self.group, 2)
        if self.group > 1:
            self.slots = [[self.group + s - o for o in self.offsets] for s in range(self.group)]
        else:
            self.slots = [[self.distances.index(-o) for o in self.offsets]]


def chunks_of(heads):
    first = (heads + 1) // 2
    return [(0, first), (first, heads - first)] if heads > 1 else [(0, heads)]


def busy(us):
    return pl.CostEstimate(flops=int(us * 1.1e9), bytes_accessed=int(us * 3.5e6), transcendentals=0)


def dot(a, b, ca, cb):
    return lax.dot_general(a, b, (((ca,), (cb,)), ((), ())), preferred_element_type=f32)


def attend(place, *refs, plan, first, heads, going_on):
    group, nd, noff = plan.group, len(plan.distances), len(plan.offsets)
    it = iter(refs)
    packs = group // plan.pack

    def unpacked():
        return [ref.at[i] for ref in [next(it) for _ in range(packs)] for i in range(plan.pack)]

    qd = [next(it) for _ in range(group)]
    kv = [unpacked() for _ in range(nd)]
    for _ in range(group if going_on else 0):
        next(it)
    out_oq = [next(it) for _ in range(group)]
    out_kv = [next(it) for _ in range(nd)]
    keys, vals, queries, grads, weights, scored, outs, dqs, allow = (next(it) for _ in range(9))
    r = place[0]

    def rows(slot):
        if isinstance(slot, int):
            return pl.ds(slot * HEAD, HEAD)
        return pl.ds(pl.multiple_of(slot * HEAD, HEAD), HEAD)

    def one_head(h, _):
        source = pl.ds(pl.multiple_of((first + h) * HEAD, HEAD), HEAD)
        target = pl.ds(pl.multiple_of(h * HEAD, HEAD), HEAD)
        for m in range(group):
            at = rows(m ^ r)
            queries[at, :] = qd[m][0:HEAD, source]
            grads[at, :] = qd[m][HEAD : 2 * HEAD, source]
            allow[m ^ r] = qd[m][2 * HEAD : 2 * HEAD + TAIL, source].astype(f32)
            for d in range(nd):
                at = rows(d * group + (m ^ r))
                keys[at, :] = kv[d][m][0, :, source]
                vals[at, :] = kv[d][m][1, :, source]

        def rows_of(j):
            return slice(j * HEAD, (j + 1) * HEAD)

        spans = range(group)
        q = [queries[rows(s), :] for s in spans]
        g = [grads[rows(s), :] for s in spans]
        k = [jnp.concatenate([keys[rows(x), :] for x in plan.slots[s]], axis=0) for s in spans]
        v = [jnp.concatenate([vals[rows(x), :] for x in plan.slots[s]], axis=0) for s in spans]
        raw = [dot(q[s], k[s], 1, 1) for s in spans]
        dp = [dot(g[s], v[s], 1, 1) for s in spans]
        p = []
        for s in spans:
            bias = jnp.concatenate([allow[s, j : j + 1, :] for j in range(noff)], axis=1)
            scores = raw[s] * (SCALE * LOG2E) + bias
            e = jnp.exp2(scores - jnp.max(scores, axis=1, keepdims=True))
            p.append(e * (1.0 / jnp.sum(e, axis=1, keepdims=True)))
        low = [x.astype(bf16) for x in p]
        o = [dot(low[s], v[s], 1, 0).astype(bf16) for s in spans]
        ds = []
        for s in spans:
            delta = jnp.sum(g[s].astype(f32) * o[s].astype(f32), axis=1, keepdims=True)
            ds.append((p[s] * SCALE * (dp[s] - delta)).astype(bf16))
        for s in spans:
            outs[rows(s), :] = o[s]
            dqs[rows(s), :] = dot(ds[s], k[s], 1, 0).astype(bf16)

        for m in range(group):
            out_oq[m][0, :, source] = outs[rows(m ^ r), :]
            out_oq[m][1, :, source] = dqs[rows(m ^ r), :]

        for d in range(nd):
            for s in range(group):
                users = [
                    (t, j)
                    for t in range(group)
                    for j in range(noff)
                    if plan.slots[t][j] == d * group + s
                ]

                def stacked(values):
                    return jnp.concatenate([values[t][:, rows_of(j)] for t, j in users], axis=0)

                qs = jnp.concatenate([q[t] for t, _ in users], axis=0)
                gs = jnp.concatenate([g[t] for t, _ in users], axis=0)
                out_kv[d][s ^ r, 1, :, target] = dot(stacked(ds), qs, 0, 0).astype(out_kv[d].dtype)
                out_kv[d][s ^ r, 0, :, target] = dot(stacked(low), gs, 0, 0).astype(out_kv[d].dtype)
        return 0

    lax.fori_loop(0, heads, one_head, 0)


def attention(place, qd, kv, oq, plan, first, heads):
    width = heads * HEAD
    group, nd, noff = plan.group, len(plan.distances), len(plan.offsets)
    ng = nd * group
    packs = group // plan.pack
    query = pl.BlockSpec((2 * HEAD + TAIL, HEAD), lambda h, _: (0, h + first))
    keyed = pl.BlockSpec((plan.pack, 2, HEAD, HEAD), lambda h, _: (0, 0, 0, h + first))
    packs = group // plan.pack
    whole = pl.BlockSpec(memory_space=pltpu.VMEM)
    args = [place, *qd, *[pack for block in kv for pack in block]]
    used = len(args)
    args += [] if oq is None else oq
    outs = [jax.ShapeDtypeStruct((2, HEAD, plan.heads * HEAD), bf16)] * group + [
        jax.ShapeDtypeStruct((group, 2, HEAD, width), f32 if by == 0 else bf16)
        for by in plan.distances
    ]
    result = pl.pallas_call(
        functools.partial(
            attend, plan=plan, first=first, heads=heads, going_on=oq is not None
        ),
        grid_spec=pltpu.PrefetchScalarGridSpec(
            num_scalar_prefetch=1,
            grid=(),
            in_specs=[whole] * (len(args) - 1),
            out_specs=[whole] * (group + nd),
            scratch_shapes=[pltpu.VMEM((ng * HEAD, HEAD), bf16)] * 2
            + [pltpu.VMEM((group * HEAD, HEAD), bf16)] * 2
            + [pltpu.VMEM((group * HEAD, noff * HEAD), bf16)] * 2
            + [pltpu.VMEM((group * HEAD, HEAD), bf16)] * 2
            + [pltpu.VMEM((group, TAIL, HEAD), f32)],
        ),
        out_shape=outs,
        compiler_params=pltpu.CompilerParams(vmem_limit_bytes=36 * 2**20),
        input_output_aliases={} if oq is None else {used + m: m for m in range(group)},
        cost_estimate=busy(4 * heads),
        name="attend",
    )(*args)
    return result[:group], result[group:]


def join(place, *refs, plan, chunks):
    group = plan.group
    count = len(chunks) * group
    parts = refs[:count]
    raw_ref, rstd_ref, gain_ref, plain, normed, inner = refs[count:]
    r = place[0]
    column = jnp.transpose(jnp.broadcast_to(rstd_ref[...], (HEAD, HEAD)))[:, 0:1]
    width = plan.heads * HEAD
    total = jnp.zeros((HEAD, HEAD), f32)
    for c, (first, heads) in enumerate(chunks):
        for m in range(group):
            base = (m ^ r) * width + first * HEAD
            part = parts[c * group + m]
            for h in range(heads):
                at = pl.ds(pl.multiple_of(base + h * HEAD, HEAD), HEAD)
                here = slice(h * HEAD, (h + 1) * HEAD)
                plain[:, at] = part[0, :, here]
                low = part[1, :, here]
                normed[:, at] = low
                total += low.astype(f32) * gain_ref[:, at] * raw_ref[:, at].astype(f32)
    inner[...] = jnp.broadcast_to(
        jnp.sum(total, axis=1, keepdims=True) * column, (HEAD, HEAD)
    )


def joined(place, parts, raw, rstd, gain, plan, chunks):
    shape = raw.shape
    flat = [x for chunk in parts for x in chunk]
    whole = pl.BlockSpec(memory_space=pltpu.VMEM)
    return pl.pallas_call(
        functools.partial(join, plan=plan, chunks=chunks),
        grid_spec=pltpu.PrefetchScalarGridSpec(
            num_scalar_prefetch=1,
            grid=(),
            in_specs=[whole] * (len(flat) + 3),
            out_specs=[whole] * 3,
        ),
        out_shape=[
            jax.ShapeDtypeStruct(shape, bf16),
            jax.ShapeDtypeStruct(shape, bf16),
            jax.ShapeDtypeStruct((HEAD, HEAD), f32),
        ],
        compiler_params=pltpu.CompilerParams(vmem_limit_bytes=24 * 2**20),
        cost_estimate=busy(2),
        name="join",
    )(place, *flat, raw, rstd, gain)


def local(
    query_vectors,
    key_vectors,
    value_vectors,
    output_grad,
    query_gain,
    key_gain,
    block_pairs,
    pair_counts,
    *,
    plan,
):
    row_count, col_count = query_vectors.shape
    group, offsets, distances = plan.group, plan.offsets, plan.distances
    features = col_count * lax.axis_size("head")
    width = col_count // group
    blocks = lax.axis_size("block")
    r = lax.axis_index("place")
    place = jnp.reshape(r, (1,)).astype(jnp.int32)

    def swap(x, m):
        return lax.ppermute(x, "place", [(i, i ^ m) for i in range(group)]) if m else x

    def moved(x, by):
        if by == 0:
            return x
        return lax.ppermute(
            x, "block", [(i, i + by) for i in range(blocks) if 0 <= i + by < blocks]
        )

    def summed(x):
        step, count = 1, lax.axis_size("head")
        while step < count:
            x = x + lax.ppermute(x, "head", [(i, i ^ step) for i in range(count)])
            step *= 2
        return x

    query_gain = query_gain[None, :]
    key_gain = key_gain[None, :]

    def chunk(x, m):
        return lax.dynamic_slice_in_dim(x, (r ^ m) * width, width, axis=1)

    squares = summed(
        jnp.stack([jnp.sum(jnp.square(x.astype(f32)), axis=1) for x in (key_vectors, query_vectors)])
    )
    my_rstd = lax.rsqrt(squares / features + epsilon)

    def normed(x, rstd, gain):
        return (x.astype(f32) * rstd[:, None] * gain).astype(bf16)

    key_norm = normed(key_vectors, my_rstd[0], key_gain)
    kv = [jnp.stack([chunk(key_norm, m), chunk(value_vectors, m)]) for m in range(group)]
    query_norm = normed(query_vectors, my_rstd[1], query_gain)
    live = jnp.arange(block_pairs.shape[1], dtype=jnp.int32) < pair_counts[0]
    steps = block_pairs[0, :, 0] - block_pairs[0, :, 1]
    wanted = jnp.array(offsets, jnp.int32)
    flags = jnp.any(live[:, None] & (steps[:, None] == wanted[None, :]), axis=0)
    bias = jnp.pad(jnp.where(flags, 0.0, lowest), (0, TAIL - len(offsets)))
    allow = jnp.broadcast_to(bias[:, None], (TAIL, width)).astype(bf16)
    qd = [
        jnp.concatenate([chunk(query_norm, m), chunk(output_grad, m), allow]) for m in range(group)
    ]

    kv = [swap(x, m) for m, x in enumerate(kv)]
    near = jnp.stack(kv[: plan.pack])
    near = [moved(near, -by) for by in distances]
    kv, qd = lax.optimization_barrier((kv, qd))
    qd = [swap(x, m) for m, x in enumerate(qd)]
    packs = [jnp.stack(kv[i : i + plan.pack]) for i in range(plan.pack, group, plan.pack)]
    packs, near, qd[group // 2 % group] = lax.optimization_barrier((packs, near, qd[group // 2 % group]))
    kv = [[x] + [moved(y, -by) for y in packs] for x, by in zip(near, distances)]

    oq = None
    back = []
    for first, count in plan.chunks:
        oq, kv_parts = attention(place, qd, kv, oq, plan, first, count)
        sent = [moved(kv_parts[d], by) for d, by in enumerate(distances) if by]
        back.append((kv_parts[plan.home], sent))
    oq = [swap(x, m) for m, x in enumerate(oq)]
    attended, query_norm_grad, query_inner = joined(
        place, [oq], query_vectors, my_rstd[1:2], query_gain, plan, [(0, plan.heads)]
    )
    kv_back = []
    for own, sent in back:
        if kv_back:
            sent, kv_back[-1] = lax.optimization_barrier((sent, kv_back[-1]))
        total = []
        for m in range(group):
            x = own[m]
            for y in sent:
                x = x + y[m].astype(f32)
            total.append(swap(x.astype(bf16), m))
        kv_back.append(total)
    value_grad, key_norm_grad, key_inner = joined(
        place, kv_back, key_vectors, my_rstd[0:1], key_gain, plan, plan.chunks
    )

    def finished(raw, rstd, gain, grad, inner):
        inner = summed(inner[:, 0])[:, None] / features
        rstd_col = rstd[0][:, None]
        unit = raw.astype(f32) * rstd_col
        return (rstd_col * (gain * grad.astype(f32) - unit * inner)).astype(bf16)

    query_grad = finished(query_vectors, my_rstd[1:2], query_gain, query_norm_grad, query_inner)
    key_grad = finished(key_vectors, my_rstd[0:1], key_gain, key_norm_grad, key_inner)
    return (attended, query_grad, key_grad, value_grad)


def solution(mesh):
    spans, head_groups = mesh.devices.shape
    plan = Plan(spans, DIM // HEAD // head_groups)
    blocks = Mesh(
        mesh.devices.reshape(spans // plan.group, plan.group, head_groups),
        ("block", "place", "head"),
    )
    ctx = ("block", "place")
    placed = (
        P(ctx, "head"),
        P(ctx, "head"),
        P(ctx, "head"),
        P(ctx, "head"),
        P("head"),
        P("head"),
        P(ctx, None, None),
        P(ctx),
    )
    return jax.shard_map(
        functools.partial(local, plan=plan),
        mesh=blocks,
        in_specs=placed,
        out_specs=(P(ctx, "head"),) * 4,
        check_vma=False,
    )
```

```python
import functools

import jax
import jax.numpy as jnp
import numpy as np
from jax import lax
from jax.experimental import pallas as pl
from jax.experimental.pallas import tpu as pltpu
from jax.sharding import Mesh
from jax.sharding import PartitionSpec as P

DIM = 5120
HEAD = 128
TAIL = 16
epsilon = 1e-06
lowest = -1e30
LOG2E = 1.4426950408889634
SCALE = HEAD ** (-0.5)
bf16 = jnp.bfloat16
f32 = jnp.float32
WIDE = pltpu.CompilerParams(vmem_limit_bytes=60 * 2**20)


def offset_list(levels):
    result = [0]
    for height in range(levels):
        result = result + [2**height, -(2**height)]
    return result


class Plan:
    def __init__(self, spans, heads_here):
        levels = spans.bit_length() - 2
        reach = 2 ** (levels - 1)
        whole = reach == 4 and heads_here % reach == 0 and spans % reach == 0
        self.group = reach if whole else 1
        self.offsets = sorted(offset_list(levels), reverse=True)
        self.distances = [-1, 0, 1] if self.group > 1 else sorted(self.offsets)
        self.home = self.distances.index(0)
        self.heads = heads_here // self.group
        self.chunks = chunks_of(self.heads)
        if self.group > 1:
            self.slots = [[self.group + s - o for o in self.offsets] for s in range(self.group)]
        else:
            self.slots = [[self.distances.index(-o) for o in self.offsets]]


def chunks_of(heads):
    first = (heads + 1) // 2
    return [(0, first), (first, heads - first)] if heads > 1 else [(0, heads)]


def busy(us):
    return pl.CostEstimate(flops=int(us * 1.1e9), bytes_accessed=int(us * 3.5e6), transcendentals=0)


def dot(a, b, ca, cb):
    return lax.dot_general(a, b, (((ca,), (cb,)), ((), ())), preferred_element_type=f32)


def attend(place, *refs, plan, first, heads):
    group, nd, noff = plan.group, len(plan.distances), len(plan.offsets)
    it = iter(refs)
    qd = [next(it) for _ in range(group)]
    kv = [[ref.at[m] for m in range(group)] for ref in [next(it) for _ in range(nd)]]
    out_oq = [next(it) for _ in range(group)]
    out_kv = [next(it) for _ in range(nd)]
    keys, vals, queries, grads, weights, scored, outs, dqs, allow = (next(it) for _ in range(9))
    r = place[0]

    def rows(slot):
        if isinstance(slot, int):
            return pl.ds(slot * HEAD, HEAD)
        return pl.ds(pl.multiple_of(slot * HEAD, HEAD), HEAD)

    def one_head(h, _):
        source = pl.ds(pl.multiple_of(h * HEAD, HEAD), HEAD)
        target = source
        for m in range(group):
            at = rows(m ^ r)
            queries[at, :] = qd[m][0:HEAD, source]
            grads[at, :] = qd[m][HEAD : 2 * HEAD, source]
            allow[m ^ r] = qd[m][2 * HEAD : 2 * HEAD + TAIL, source].astype(f32)
            for d in range(nd):
                at = rows(d * group + (m ^ r))
                keys[at, :] = kv[d][m][0, :, source]
                vals[at, :] = kv[d][m][1, :, source]

        def rows_of(j):
            return slice(j * HEAD, (j + 1) * HEAD)

        spans = range(group)
        q = [queries[rows(s), :] for s in spans]
        g = [grads[rows(s), :] for s in spans]
        k = [jnp.concatenate([keys[rows(x), :] for x in plan.slots[s]], axis=0) for s in spans]
        v = [jnp.concatenate([vals[rows(x), :] for x in plan.slots[s]], axis=0) for s in spans]
        raw = [dot(q[s], k[s], 1, 1) for s in spans]
        dp = [dot(g[s], v[s], 1, 1) for s in spans]
        p = []
        for s in spans:
            bias = jnp.concatenate([allow[s, j : j + 1, :] for j in range(noff)], axis=1)
            scores = raw[s] * (SCALE * LOG2E) + bias
            e = jnp.exp2(scores - jnp.max(scores, axis=1, keepdims=True))
            p.append(e * (1.0 / jnp.sum(e, axis=1, keepdims=True)))
        low = [x.astype(bf16) for x in p]
        o = [dot(low[s], v[s], 1, 0).astype(bf16) for s in spans]
        ds = []
        for s in spans:
            delta = jnp.sum(g[s].astype(f32) * o[s].astype(f32), axis=1, keepdims=True)
            ds.append((p[s] * SCALE * (dp[s] - delta)).astype(bf16))
        for s in spans:
            outs[rows(s), :] = o[s]
            dqs[rows(s), :] = dot(ds[s], k[s], 1, 0).astype(bf16)

        for m in range(group):
            out_oq[m][0, :, target] = outs[rows(m ^ r), :]
            out_oq[m][1, :, target] = dqs[rows(m ^ r), :]

        for d in range(nd):
            for s in range(group):
                users = [
                    (t, j)
                    for t in range(group)
                    for j in range(noff)
                    if plan.slots[t][j] == d * group + s
                ]

                def stacked(values):
                    return jnp.concatenate([values[t][:, rows_of(j)] for t, j in users], axis=0)

                qs = jnp.concatenate([q[t] for t, _ in users], axis=0)
                gs = jnp.concatenate([g[t] for t, _ in users], axis=0)
                out_kv[d][s ^ r, 1, :, target] = dot(stacked(ds), qs, 0, 0).astype(out_kv[d].dtype)
                out_kv[d][s ^ r, 0, :, target] = dot(stacked(low), gs, 0, 0).astype(out_kv[d].dtype)
        return 0

    lax.fori_loop(0, heads, one_head, 0)


def attention(place, qd, kv, plan, first, heads):
    width = heads * HEAD
    group, nd, noff = plan.group, len(plan.distances), len(plan.offsets)
    ng = nd * group
    whole = pl.BlockSpec(memory_space=pltpu.VMEM)
    args = [place, *qd, *kv]
    outs = [jax.ShapeDtypeStruct((2, HEAD, width), bf16)] * group + [
        jax.ShapeDtypeStruct((group, 2, HEAD, width), f32 if by == 0 else bf16)
        for by in plan.distances
    ]
    result = pl.pallas_call(
        functools.partial(attend, plan=plan, first=first, heads=heads),
        grid_spec=pltpu.PrefetchScalarGridSpec(
            num_scalar_prefetch=1,
            grid=(),
            in_specs=[whole] * (len(args) - 1),
            out_specs=[whole] * (group + nd),
            scratch_shapes=[pltpu.VMEM((ng * HEAD, HEAD), bf16)] * 2
            + [pltpu.VMEM((group * HEAD, HEAD), bf16)] * 2
            + [pltpu.VMEM((group * HEAD, noff * HEAD), bf16)] * 2
            + [pltpu.VMEM((group * HEAD, HEAD), bf16)] * 2
            + [pltpu.VMEM((group, TAIL, HEAD), f32)],
        ),
        out_shape=outs,
        compiler_params=pltpu.CompilerParams(vmem_limit_bytes=36 * 2**20),
        cost_estimate=busy(4 * heads),
        name="attend",
    )(*args)
    return result[:group], result[group:]


def join(place, *refs, plan):
    group = plan.group
    count = len(plan.chunks) * group
    parts = refs[:count]
    raw_ref, rstd_ref, gain_ref, plain, normed, inner = refs[count:]
    r = place[0]
    column = jnp.transpose(jnp.broadcast_to(rstd_ref[...], (HEAD, HEAD)))[:, 0:1]
    width = plan.heads * HEAD
    total = jnp.zeros((HEAD, HEAD), f32)
    for c, (first, heads) in enumerate(plan.chunks):
        for m in range(group):
            base = (m ^ r) * width + first * HEAD
            part = parts[c * group + m]
            for h in range(heads):
                at = pl.ds(pl.multiple_of(base + h * HEAD, HEAD), HEAD)
                here = slice(h * HEAD, (h + 1) * HEAD)
                plain[:, at] = part[0, :, here]
                low = part[1, :, here]
                normed[:, at] = low
                total += low.astype(f32) * gain_ref[:, at] * raw_ref[:, at].astype(f32)
    inner[...] = jnp.broadcast_to(
        jnp.sum(total, axis=1, keepdims=True) * column, (HEAD, HEAD)
    )


def joined(place, parts, raw, rstd, gain, plan):
    shape = raw.shape
    flat = [x for chunk in parts for x in chunk]
    whole = pl.BlockSpec(memory_space=pltpu.VMEM)
    return pl.pallas_call(
        functools.partial(join, plan=plan),
        grid_spec=pltpu.PrefetchScalarGridSpec(
            num_scalar_prefetch=1,
            grid=(),
            in_specs=[whole] * (len(flat) + 3),
            out_specs=[whole] * 3,
        ),
        out_shape=[
            jax.ShapeDtypeStruct(shape, bf16),
            jax.ShapeDtypeStruct(shape, bf16),
            jax.ShapeDtypeStruct((HEAD, HEAD), f32),
        ],
        compiler_params=pltpu.CompilerParams(vmem_limit_bytes=24 * 2**20),
        cost_estimate=busy(2),
        name="join",
    )(place, *flat, raw, rstd, gain)


def local(
    query_vectors,
    key_vectors,
    value_vectors,
    output_grad,
    query_gain,
    key_gain,
    block_pairs,
    pair_counts,
    *,
    plan,
):
    row_count, col_count = query_vectors.shape
    group, offsets, distances = plan.group, plan.offsets, plan.distances
    features = col_count * lax.axis_size("head")
    width = col_count // group
    blocks = lax.axis_size("block")
    r = lax.axis_index("place")
    place = jnp.reshape(r, (1,)).astype(jnp.int32)

    def swap(x, m):
        return lax.ppermute(x, "place", [(i, i ^ m) for i in range(group)]) if m else x

    def moved(x, by):
        if by == 0:
            return x
        return lax.ppermute(
            x, "block", [(i, i + by) for i in range(blocks) if 0 <= i + by < blocks]
        )

    def summed(x):
        step, count = 1, lax.axis_size("head")
        while step < count:
            x = x + lax.ppermute(x, "head", [(i, i ^ step) for i in range(count)])
            step *= 2
        return x

    query_gain = query_gain[None, :]
    key_gain = key_gain[None, :]

    def chunk(x, m):
        return lax.dynamic_slice_in_dim(x, (r ^ m) * width, width, axis=1)

    squares = summed(
        jnp.stack([jnp.sum(jnp.square(x.astype(f32)), axis=1) for x in (key_vectors, query_vectors)])
    )
    my_rstd = lax.rsqrt(squares / features + epsilon)

    def normed(x, rstd, gain):
        return (x.astype(f32) * rstd[:, None] * gain).astype(bf16)

    key_norm = normed(key_vectors, my_rstd[0], key_gain)
    query_norm = normed(query_vectors, my_rstd[1], query_gain)
    live = jnp.arange(block_pairs.shape[1], dtype=jnp.int32) < pair_counts[0]
    steps = block_pairs[0, :, 0] - block_pairs[0, :, 1]
    wanted = jnp.array(offsets, jnp.int32)
    flags = jnp.any(live[:, None] & (steps[:, None] == wanted[None, :]), axis=0)
    bias = jnp.pad(jnp.where(flags, 0.0, lowest), (0, TAIL - len(offsets)))
    allow = jnp.broadcast_to(bias[:, None], (TAIL, width)).astype(bf16)

    def cut(x, m, first, count):
        return lax.dynamic_slice_in_dim(x, (r ^ m) * width + first * HEAD, count * HEAD, axis=1)

    kv_cut = [
        [jnp.stack([cut(key_norm, m, *c), cut(value_vectors, m, *c)]) for m in range(group)]
        for c in plan.chunks
    ]
    qd_cut = [
        [
            jnp.concatenate(
                [cut(query_norm, m, *c), cut(output_grad, m, *c), allow[:, : c[1] * HEAD]]
            )
            for m in range(group)
        ]
        for c in plan.chunks
    ]

    def after(x, *earlier):
        return lax.optimization_barrier((x, earlier))[0]

    def swaps(xs):
        return [swap(x, m) for m, x in enumerate(xs)]

    half, last = group // 2, group - 1
    kv, qd = [], []
    arrived = None
    for c in range(len(plan.chunks)):
        mine = kv_cut[c] if arrived is None else after(kv_cut[c], arrived[half])
        arrived = swaps(mine)
        kv.append(arrived)
    for c in range(len(plan.chunks)):
        arrived = swaps(after(qd_cut[c], arrived[half]))
        qd.append(arrived)
    halo = []
    for c in range(len(plan.chunks)):
        pack = jnp.stack(kv[c])
        if halo:
            pack = after(pack, qd[0][last])
        halo.append([moved(pack, -by) for by in distances])
    kv = halo

    back = []
    oq_back = []
    for c, (first, count) in enumerate(plan.chunks):
        oq, kv_parts = attention(place, qd[c], kv[c], plan, first, count)
        sent = [moved(kv_parts[d], by) for d, by in enumerate(distances) if by]
        back.append((kv_parts[plan.home], sent))
        oq_back.append([swap(x, m) for m, x in enumerate(oq)])
    attended, query_norm_grad, query_inner = joined(
        place, oq_back, query_vectors, my_rstd[1:2], query_gain, plan
    )
    kv_back = []
    for own, sent in back:
        if kv_back:
            sent, kv_back[-1] = lax.optimization_barrier((sent, kv_back[-1]))
        total = []
        for m in range(group):
            x = own[m]
            for y in sent:
                x = x + y[m].astype(f32)
            total.append(swap(x.astype(bf16), m))
        kv_back.append(total)
    value_grad, key_norm_grad, key_inner = joined(
        place, kv_back, key_vectors, my_rstd[0:1], key_gain, plan
    )

    def finished(raw, rstd, gain, grad, inner):
        inner = summed(inner[:, 0])[:, None] / features
        rstd_col = rstd[0][:, None]
        unit = raw.astype(f32) * rstd_col
        return (rstd_col * (gain * grad.astype(f32) - unit * inner)).astype(bf16)

    query_grad = finished(query_vectors, my_rstd[1:2], query_gain, query_norm_grad, query_inner)
    key_grad = finished(key_vectors, my_rstd[0:1], key_gain, key_norm_grad, key_inner)
    return (attended, query_grad, key_grad, value_grad)


def solution(mesh):
    spans, head_groups = mesh.devices.shape
    plan = Plan(spans, DIM // HEAD // head_groups)
    blocks = Mesh(
        mesh.devices.reshape(spans // plan.group, plan.group, head_groups),
        ("block", "place", "head"),
    )
    ctx = ("block", "place")
    placed = (
        P(ctx, "head"),
        P(ctx, "head"),
        P(ctx, "head"),
        P(ctx, "head"),
        P("head"),
        P("head"),
        P(ctx, None, None),
        P(ctx),
    )
    return jax.shard_map(
        functools.partial(local, plan=plan),
        mesh=blocks,
        in_specs=placed,
        out_specs=(P(ctx, "head"),) * 4,
        check_vma=False,
    )
```

```python
import functools

import jax
import jax.numpy as jnp
import numpy as np
from jax import lax
from jax.experimental import pallas as pl
from jax.experimental.pallas import tpu as pltpu
from jax.sharding import Mesh
from jax.sharding import PartitionSpec as P

DIM = 5120
HEAD = 128
TAIL = 16
epsilon = 1e-06
lowest = -1e30
LOG2E = 1.4426950408889634
SCALE = HEAD ** (-0.5)
bf16 = jnp.bfloat16
f32 = jnp.float32
WIDE = pltpu.CompilerParams(vmem_limit_bytes=60 * 2**20)


def offset_list(levels):
    result = [0]
    for height in range(levels):
        result = result + [2**height, -(2**height)]
    return result


class Plan:
    def __init__(self, spans, heads_here):
        levels = spans.bit_length() - 2
        reach = 2 ** (levels - 1)
        whole = reach == 4 and heads_here % reach == 0 and spans % reach == 0
        self.group = reach if whole else 1
        self.offsets = sorted(offset_list(levels), reverse=True)
        self.distances = [-1, 0, 1] if self.group > 1 else sorted(self.offsets)
        self.home = self.distances.index(0)
        self.heads = heads_here // self.group
        self.chunks = chunks_of(self.heads)
        if self.group > 1:
            self.slots = [[self.group + s - o for o in self.offsets] for s in range(self.group)]
        else:
            self.slots = [[self.distances.index(-o) for o in self.offsets]]


def chunks_of(heads):
    first = (heads + 1) // 2
    return [(0, first), (first, heads - first)] if heads > 1 else [(0, heads)]


def busy(us):
    return pl.CostEstimate(flops=int(us * 1.1e9), bytes_accessed=int(us * 3.5e6), transcendentals=0)


def dot(a, b, ca, cb):
    return lax.dot_general(a, b, (((ca,), (cb,)), ((), ())), preferred_element_type=f32)


def attend(place, *refs, plan, first, heads):
    group, nd, noff = plan.group, len(plan.distances), len(plan.offsets)
    it = iter(refs)
    qd = [next(it) for _ in range(group)]
    kv = [[ref.at[m] for m in range(group)] for ref in [next(it) for _ in range(nd)]]
    out_oq = [next(it) for _ in range(group)]
    out_kv = [next(it) for _ in range(nd)]
    keys, vals, queries, grads, weights, scored, outs, dqs, allow = (next(it) for _ in range(9))
    r = place[0]

    def rows(slot):
        if isinstance(slot, int):
            return pl.ds(slot * HEAD, HEAD)
        return pl.ds(pl.multiple_of(slot * HEAD, HEAD), HEAD)

    def one_head(h, _):
        source = pl.ds(pl.multiple_of(h * HEAD, HEAD), HEAD)
        target = source
        for m in range(group):
            at = rows(m ^ r)
            queries[at, :] = qd[m][0:HEAD, source]
            grads[at, :] = qd[m][HEAD : 2 * HEAD, source]
            allow[m ^ r] = qd[m][2 * HEAD : 2 * HEAD + TAIL, source].astype(f32)
            for d in range(nd):
                at = rows(d * group + (m ^ r))
                keys[at, :] = kv[d][m][0, :, source]
                vals[at, :] = kv[d][m][1, :, source]

        def rows_of(j):
            return slice(j * HEAD, (j + 1) * HEAD)

        spans = range(group)
        q = [queries[rows(s), :] for s in spans]
        g = [grads[rows(s), :] for s in spans]
        k = [jnp.concatenate([keys[rows(x), :] for x in plan.slots[s]], axis=0) for s in spans]
        v = [jnp.concatenate([vals[rows(x), :] for x in plan.slots[s]], axis=0) for s in spans]
        raw = [dot(q[s], k[s], 1, 1) for s in spans]
        dp = [dot(g[s], v[s], 1, 1) for s in spans]
        p = []
        for s in spans:
            bias = jnp.concatenate([allow[s, j : j + 1, :] for j in range(noff)], axis=1)
            scores = raw[s] * (SCALE * LOG2E) + bias
            e = jnp.exp2(scores - jnp.max(scores, axis=1, keepdims=True))
            p.append(e * (1.0 / jnp.sum(e, axis=1, keepdims=True)))
        low = [x.astype(bf16) for x in p]
        o = [dot(low[s], v[s], 1, 0).astype(bf16) for s in spans]
        ds = []
        for s in spans:
            delta = jnp.sum(g[s].astype(f32) * o[s].astype(f32), axis=1, keepdims=True)
            ds.append((p[s] * SCALE * (dp[s] - delta)).astype(bf16))
        for s in spans:
            outs[rows(s), :] = o[s]
            dqs[rows(s), :] = dot(ds[s], k[s], 1, 0).astype(bf16)

        for m in range(group):
            out_oq[m][0, :, target] = outs[rows(m ^ r), :]
            out_oq[m][1, :, target] = dqs[rows(m ^ r), :]

        for d in range(nd):
            for s in range(group):
                users = [
                    (t, j)
                    for t in range(group)
                    for j in range(noff)
                    if plan.slots[t][j] == d * group + s
                ]

                def stacked(values):
                    return jnp.concatenate([values[t][:, rows_of(j)] for t, j in users], axis=0)

                qs = jnp.concatenate([q[t] for t, _ in users], axis=0)
                gs = jnp.concatenate([g[t] for t, _ in users], axis=0)
                out_kv[d][s ^ r, 1, :, target] = dot(stacked(ds), qs, 0, 0).astype(out_kv[d].dtype)
                out_kv[d][s ^ r, 0, :, target] = dot(stacked(low), gs, 0, 0).astype(out_kv[d].dtype)
        return 0

    lax.fori_loop(0, heads, one_head, 0)


def attention(place, qd, kv, plan, first, heads):
    width = heads * HEAD
    group, nd, noff = plan.group, len(plan.distances), len(plan.offsets)
    ng = nd * group
    whole = pl.BlockSpec(memory_space=pltpu.VMEM)
    args = [place, *qd, *kv]
    outs = [jax.ShapeDtypeStruct((2, HEAD, width), bf16)] * group + [
        jax.ShapeDtypeStruct((group, 2, HEAD, width), f32 if by == 0 else bf16)
        for by in plan.distances
    ]
    result = pl.pallas_call(
        functools.partial(attend, plan=plan, first=first, heads=heads),
        grid_spec=pltpu.PrefetchScalarGridSpec(
            num_scalar_prefetch=1,
            grid=(),
            in_specs=[whole] * (len(args) - 1),
            out_specs=[whole] * (group + nd),
            scratch_shapes=[pltpu.VMEM((ng * HEAD, HEAD), bf16)] * 2
            + [pltpu.VMEM((group * HEAD, HEAD), bf16)] * 2
            + [pltpu.VMEM((group * HEAD, noff * HEAD), bf16)] * 2
            + [pltpu.VMEM((group * HEAD, HEAD), bf16)] * 2
            + [pltpu.VMEM((group, TAIL, HEAD), f32)],
        ),
        out_shape=outs,
        compiler_params=pltpu.CompilerParams(vmem_limit_bytes=36 * 2**20),
        cost_estimate=busy(4 * heads),
        name="attend",
    )(*args)
    return result[:group], result[group:]


def join(place, *refs, plan):
    group = plan.group
    count = len(plan.chunks) * group
    parts = refs[:count]
    raw_ref, rstd_ref, gain_ref, plain, normed, inner = refs[count:]
    r = place[0]
    column = jnp.transpose(jnp.broadcast_to(rstd_ref[...], (HEAD, HEAD)))[:, 0:1]
    width = plan.heads * HEAD
    total = jnp.zeros((HEAD, HEAD), f32)
    for c, (first, heads) in enumerate(plan.chunks):
        for m in range(group):
            base = (m ^ r) * width + first * HEAD
            part = parts[c * group + m]
            for h in range(heads):
                at = pl.ds(pl.multiple_of(base + h * HEAD, HEAD), HEAD)
                here = slice(h * HEAD, (h + 1) * HEAD)
                plain[:, at] = part[0, :, here]
                low = part[1, :, here]
                normed[:, at] = low
                total += low.astype(f32) * gain_ref[:, at] * raw_ref[:, at].astype(f32)
    inner[...] = jnp.broadcast_to(
        jnp.sum(total, axis=1, keepdims=True) * column, (HEAD, HEAD)
    )


def joined(place, parts, raw, rstd, gain, plan):
    shape = raw.shape
    flat = [x for chunk in parts for x in chunk]
    whole = pl.BlockSpec(memory_space=pltpu.VMEM)
    return pl.pallas_call(
        functools.partial(join, plan=plan),
        grid_spec=pltpu.PrefetchScalarGridSpec(
            num_scalar_prefetch=1,
            grid=(),
            in_specs=[whole] * (len(flat) + 3),
            out_specs=[whole] * 3,
        ),
        out_shape=[
            jax.ShapeDtypeStruct(shape, bf16),
            jax.ShapeDtypeStruct(shape, bf16),
            jax.ShapeDtypeStruct((HEAD, HEAD), f32),
        ],
        compiler_params=pltpu.CompilerParams(vmem_limit_bytes=24 * 2**20),
        cost_estimate=busy(2),
        name="join",
    )(place, *flat, raw, rstd, gain)


def local(
    query_vectors,
    key_vectors,
    value_vectors,
    output_grad,
    query_gain,
    key_gain,
    block_pairs,
    pair_counts,
    *,
    plan,
):
    row_count, col_count = query_vectors.shape
    group, offsets, distances = plan.group, plan.offsets, plan.distances
    features = col_count * lax.axis_size("head")
    width = col_count // group
    blocks = lax.axis_size("block")
    r = lax.axis_index("place")
    place = jnp.reshape(r, (1,)).astype(jnp.int32)

    def swap(x, m):
        return lax.ppermute(x, "place", [(i, i ^ m) for i in range(group)]) if m else x

    def moved(x, by):
        if by == 0:
            return x
        return lax.ppermute(
            x, "block", [(i, i + by) for i in range(blocks) if 0 <= i + by < blocks]
        )

    def summed(x):
        step, count = 1, lax.axis_size("head")
        while step < count:
            x = x + lax.ppermute(x, "head", [(i, i ^ step) for i in range(count)])
            step *= 2
        return x

    query_gain = query_gain[None, :]
    key_gain = key_gain[None, :]

    def chunk(x, m):
        return lax.dynamic_slice_in_dim(x, (r ^ m) * width, width, axis=1)

    squares = summed(
        jnp.stack([jnp.sum(jnp.square(x.astype(f32)), axis=1) for x in (key_vectors, query_vectors)])
    )
    my_rstd = lax.rsqrt(squares / features + epsilon)

    def normed(x, rstd, gain):
        return (x.astype(f32) * rstd[:, None] * gain).astype(bf16)

    key_norm = normed(key_vectors, my_rstd[0], key_gain)
    query_norm = normed(query_vectors, my_rstd[1], query_gain)
    live = jnp.arange(block_pairs.shape[1], dtype=jnp.int32) < pair_counts[0]
    steps = block_pairs[0, :, 0] - block_pairs[0, :, 1]
    wanted = jnp.array(offsets, jnp.int32)
    flags = jnp.any(live[:, None] & (steps[:, None] == wanted[None, :]), axis=0)
    bias = jnp.pad(jnp.where(flags, 0.0, lowest), (0, TAIL - len(offsets)))
    allow = jnp.broadcast_to(bias[:, None], (TAIL, width)).astype(bf16)

    def cut(x, m, first, count):
        return lax.dynamic_slice_in_dim(x, (r ^ m) * width + first * HEAD, count * HEAD, axis=1)

    kv_cut = [
        [jnp.stack([cut(key_norm, m, *c), cut(value_vectors, m, *c)]) for m in range(group)]
        for c in plan.chunks
    ]
    qd_cut = [
        [
            jnp.concatenate(
                [cut(query_norm, m, *c), cut(output_grad, m, *c), allow[:, : c[1] * HEAD]]
            )
            for m in range(group)
        ]
        for c in plan.chunks
    ]

    def after(x, *earlier):
        return lax.optimization_barrier((x, earlier))[0]

    def swaps(xs):
        return [swap(x, m) for m, x in enumerate(xs)]

    half, last = group // 2, group - 1
    kv, qd = [], []
    arrived = None
    for c in range(len(plan.chunks)):
        mine = kv_cut[c] if arrived is None else after(kv_cut[c], arrived[half])
        arrived = swaps(mine)
        kv.append(arrived)
    for c in range(len(plan.chunks)):
        arrived = swaps(after(qd_cut[c], arrived[half]))
        qd.append(arrived)
    halo = []
    for c in range(len(plan.chunks)):
        pack = jnp.stack(kv[c])
        if halo:
            pack = after(pack, qd[0][1 % group])
        halo.append([moved(pack, -by) for by in distances])
    kv = halo

    back = []
    oq_back = []
    for c, (first, count) in enumerate(plan.chunks):
        oq, kv_parts = attention(place, qd[c], kv[c], plan, first, count)
        sent = [moved(kv_parts[d], by) for d, by in enumerate(distances) if by]
        back.append((kv_parts[plan.home], sent))
        oq_back.append([swap(x, m) for m, x in enumerate(oq)])
    attended, query_norm_grad, query_inner = joined(
        place, oq_back, query_vectors, my_rstd[1:2], query_gain, plan
    )
    kv_back = []
    for own, sent in back:
        if kv_back:
            sent, kv_back[-1] = lax.optimization_barrier((sent, kv_back[-1]))
        total = []
        for m in range(group):
            x = own[m]
            for y in sent:
                x = x + y[m].astype(f32)
            total.append(swap(x.astype(bf16), m))
        kv_back.append(total)
    value_grad, key_norm_grad, key_inner = joined(
        place, kv_back, key_vectors, my_rstd[0:1], key_gain, plan
    )

    def finished(raw, rstd, gain, grad, inner):
        inner = summed(inner[:, 0])[:, None] / features
        rstd_col = rstd[0][:, None]
        unit = raw.astype(f32) * rstd_col
        return (rstd_col * (gain * grad.astype(f32) - unit * inner)).astype(bf16)

    query_grad = finished(query_vectors, my_rstd[1:2], query_gain, query_norm_grad, query_inner)
    key_grad = finished(key_vectors, my_rstd[0:1], key_gain, key_norm_grad, key_inner)
    return (attended, query_grad, key_grad, value_grad)


def solution(mesh):
    spans, head_groups = mesh.devices.shape
    plan = Plan(spans, DIM // HEAD // head_groups)
    blocks = Mesh(
        mesh.devices.reshape(spans // plan.group, plan.group, head_groups),
        ("block", "place", "head"),
    )
    ctx = ("block", "place")
    placed = (
        P(ctx, "head"),
        P(ctx, "head"),
        P(ctx, "head"),
        P(ctx, "head"),
        P("head"),
        P("head"),
        P(ctx, None, None),
        P(ctx),
    )
    return jax.shard_map(
        functools.partial(local, plan=plan),
        mesh=blocks,
        in_specs=placed,
        out_specs=(P(ctx, "head"),) * 4,
        check_vma=False,
    )
```

```python
import functools

import jax
import jax.numpy as jnp
import numpy as np
from jax import lax
from jax.experimental import pallas as pl
from jax.experimental.pallas import tpu as pltpu
from jax.sharding import Mesh
from jax.sharding import PartitionSpec as P

DIM = 5120
HEAD = 128
TAIL = 16
epsilon = 1e-06
lowest = -1e30
LOG2E = 1.4426950408889634
SCALE = HEAD ** (-0.5)
bf16 = jnp.bfloat16
f32 = jnp.float32
WIDE = pltpu.CompilerParams(vmem_limit_bytes=60 * 2**20)


def offset_list(levels):
    result = [0]
    for height in range(levels):
        result = result + [2**height, -(2**height)]
    return result


class Plan:
    def __init__(self, spans, heads_here):
        levels = spans.bit_length() - 2
        reach = 2 ** (levels - 1)
        whole = reach == 4 and heads_here % reach == 0 and spans % reach == 0
        self.group = reach if whole else 1
        self.offsets = sorted(offset_list(levels), reverse=True)
        self.distances = [-1, 0, 1] if self.group > 1 else sorted(self.offsets)
        self.home = self.distances.index(0)
        self.heads = heads_here // self.group
        self.chunks = chunks_of(self.heads)
        if self.group > 1:
            self.slots = [[self.group + s - o for o in self.offsets] for s in range(self.group)]
        else:
            self.slots = [[self.distances.index(-o) for o in self.offsets]]


def chunks_of(heads):
    first = (heads + 1) // 2
    return [(0, first), (first, heads - first)] if heads > 1 else [(0, heads)]


def busy(us):
    return pl.CostEstimate(flops=int(us * 1.1e9), bytes_accessed=int(us * 3.5e6), transcendentals=0)


def dot(a, b, ca, cb):
    return lax.dot_general(a, b, (((ca,), (cb,)), ((), ())), preferred_element_type=f32)


def attend(place, *refs, plan, first, heads):
    group, nd, noff = plan.group, len(plan.distances), len(plan.offsets)
    it = iter(refs)
    qd = [next(it) for _ in range(group)]
    kv = [[ref.at[m] for m in range(group)] for ref in [next(it) for _ in range(nd)]]
    out_oq = [next(it) for _ in range(group)]
    out_kv = [next(it) for _ in range(nd)]
    keys, vals, queries, grads, weights, scored, outs, dqs, allow = (next(it) for _ in range(9))
    r = place[0]

    def rows(slot):
        if isinstance(slot, int):
            return pl.ds(slot * HEAD, HEAD)
        return pl.ds(pl.multiple_of(slot * HEAD, HEAD), HEAD)

    def one_head(h, _):
        source = pl.ds(pl.multiple_of(h * HEAD, HEAD), HEAD)
        target = source
        for m in range(group):
            at = rows(m ^ r)
            queries[at, :] = qd[m][0:HEAD, source]
            grads[at, :] = qd[m][HEAD : 2 * HEAD, source]
            allow[m ^ r] = qd[m][2 * HEAD : 2 * HEAD + TAIL, source].astype(f32)
            for d in range(nd):
                at = rows(d * group + (m ^ r))
                keys[at, :] = kv[d][m][0, :, source]
                vals[at, :] = kv[d][m][1, :, source]

        def rows_of(j):
            return slice(j * HEAD, (j + 1) * HEAD)

        spans = range(group)
        q = [queries[rows(s), :] for s in spans]
        g = [grads[rows(s), :] for s in spans]
        k = [jnp.concatenate([keys[rows(x), :] for x in plan.slots[s]], axis=0) for s in spans]
        v = [jnp.concatenate([vals[rows(x), :] for x in plan.slots[s]], axis=0) for s in spans]
        raw = [dot(q[s], k[s], 1, 1) for s in spans]
        dp = [dot(g[s], v[s], 1, 1) for s in spans]
        p = []
        for s in spans:
            bias = jnp.concatenate([allow[s, j : j + 1, :] for j in range(noff)], axis=1)
            scores = raw[s] * (SCALE * LOG2E) + bias
            e = jnp.exp2(scores - jnp.max(scores, axis=1, keepdims=True))
            p.append(e * (1.0 / jnp.sum(e, axis=1, keepdims=True)))
        low = [x.astype(bf16) for x in p]
        o = [dot(low[s], v[s], 1, 0).astype(bf16) for s in spans]
        ds = []
        for s in spans:
            delta = jnp.sum(g[s].astype(f32) * o[s].astype(f32), axis=1, keepdims=True)
            ds.append((p[s] * SCALE * (dp[s] - delta)).astype(bf16))
        for s in spans:
            outs[rows(s), :] = o[s]
            dqs[rows(s), :] = dot(ds[s], k[s], 1, 0).astype(bf16)

        for m in range(group):
            out_oq[m][0, :, target] = outs[rows(m ^ r), :]
            out_oq[m][1, :, target] = dqs[rows(m ^ r), :]

        for d in range(nd):
            for s in range(group):
                users = [
                    (t, j)
                    for t in range(group)
                    for j in range(noff)
                    if plan.slots[t][j] == d * group + s
                ]

                def stacked(values):
                    return jnp.concatenate([values[t][:, rows_of(j)] for t, j in users], axis=0)

                qs = jnp.concatenate([q[t] for t, _ in users], axis=0)
                gs = jnp.concatenate([g[t] for t, _ in users], axis=0)
                out_kv[d][s ^ r, 1, :, target] = dot(stacked(ds), qs, 0, 0).astype(out_kv[d].dtype)
                out_kv[d][s ^ r, 0, :, target] = dot(stacked(low), gs, 0, 0).astype(out_kv[d].dtype)
        return 0

    lax.fori_loop(0, heads, one_head, 0)


def attention(place, qd, kv, plan, first, heads):
    width = heads * HEAD
    group, nd, noff = plan.group, len(plan.distances), len(plan.offsets)
    ng = nd * group
    whole = pl.BlockSpec(memory_space=pltpu.VMEM)
    args = [place, *qd, *kv]
    outs = [jax.ShapeDtypeStruct((2, HEAD, width), bf16)] * group + [
        jax.ShapeDtypeStruct((group, 2, HEAD, width), f32 if by == 0 else bf16)
        for by in plan.distances
    ]
    result = pl.pallas_call(
        functools.partial(attend, plan=plan, first=first, heads=heads),
        grid_spec=pltpu.PrefetchScalarGridSpec(
            num_scalar_prefetch=1,
            grid=(),
            in_specs=[whole] * (len(args) - 1),
            out_specs=[whole] * (group + nd),
            scratch_shapes=[pltpu.VMEM((ng * HEAD, HEAD), bf16)] * 2
            + [pltpu.VMEM((group * HEAD, HEAD), bf16)] * 2
            + [pltpu.VMEM((group * HEAD, noff * HEAD), bf16)] * 2
            + [pltpu.VMEM((group * HEAD, HEAD), bf16)] * 2
            + [pltpu.VMEM((group, TAIL, HEAD), f32)],
        ),
        out_shape=outs,
        compiler_params=pltpu.CompilerParams(vmem_limit_bytes=36 * 2**20),
        cost_estimate=busy(10 * heads),
        name="attend",
    )(*args)
    return result[:group], result[group:]


def join(place, *refs, plan):
    group = plan.group
    count = len(plan.chunks) * group
    parts = refs[:count]
    raw_ref, rstd_ref, gain_ref, plain, normed, inner = refs[count:]
    r = place[0]
    column = jnp.transpose(jnp.broadcast_to(rstd_ref[...], (HEAD, HEAD)))[:, 0:1]
    width = plan.heads * HEAD
    total = jnp.zeros((HEAD, HEAD), f32)
    for c, (first, heads) in enumerate(plan.chunks):
        for m in range(group):
            base = (m ^ r) * width + first * HEAD
            part = parts[c * group + m]
            for h in range(heads):
                at = pl.ds(pl.multiple_of(base + h * HEAD, HEAD), HEAD)
                here = slice(h * HEAD, (h + 1) * HEAD)
                plain[:, at] = part[0, :, here]
                low = part[1, :, here]
                normed[:, at] = low
                total += low.astype(f32) * gain_ref[:, at] * raw_ref[:, at].astype(f32)
    inner[...] = jnp.broadcast_to(
        jnp.sum(total, axis=1, keepdims=True) * column, (HEAD, HEAD)
    )


def joined(place, parts, raw, rstd, gain, plan):
    shape = raw.shape
    flat = [x for chunk in parts for x in chunk]
    whole = pl.BlockSpec(memory_space=pltpu.VMEM)
    return pl.pallas_call(
        functools.partial(join, plan=plan),
        grid_spec=pltpu.PrefetchScalarGridSpec(
            num_scalar_prefetch=1,
            grid=(),
            in_specs=[whole] * (len(flat) + 3),
            out_specs=[whole] * 3,
        ),
        out_shape=[
            jax.ShapeDtypeStruct(shape, bf16),
            jax.ShapeDtypeStruct(shape, bf16),
            jax.ShapeDtypeStruct((HEAD, HEAD), f32),
        ],
        compiler_params=pltpu.CompilerParams(vmem_limit_bytes=24 * 2**20),
        cost_estimate=busy(2),
        name="join",
    )(place, *flat, raw, rstd, gain)


def local(
    query_vectors,
    key_vectors,
    value_vectors,
    output_grad,
    query_gain,
    key_gain,
    block_pairs,
    pair_counts,
    *,
    plan,
):
    row_count, col_count = query_vectors.shape
    group, offsets, distances = plan.group, plan.offsets, plan.distances
    features = col_count * lax.axis_size("head")
    width = col_count // group
    blocks = lax.axis_size("block")
    r = lax.axis_index("place")
    place = jnp.reshape(r, (1,)).astype(jnp.int32)

    def swap(x, m):
        return lax.ppermute(x, "place", [(i, i ^ m) for i in range(group)]) if m else x

    def moved(x, by):
        if by == 0:
            return x
        return lax.ppermute(
            x, "block", [(i, i + by) for i in range(blocks) if 0 <= i + by < blocks]
        )

    def summed(x):
        step, count = 1, lax.axis_size("head")
        while step < count:
            x = x + lax.ppermute(x, "head", [(i, i ^ step) for i in range(count)])
            step *= 2
        return x

    query_gain = query_gain[None, :]
    key_gain = key_gain[None, :]

    def chunk(x, m):
        return lax.dynamic_slice_in_dim(x, (r ^ m) * width, width, axis=1)

    squares = summed(
        jnp.stack([jnp.sum(jnp.square(x.astype(f32)), axis=1) for x in (key_vectors, query_vectors)])
    )
    my_rstd = lax.rsqrt(squares / features + epsilon)

    def normed(x, rstd, gain):
        return (x.astype(f32) * rstd[:, None] * gain).astype(bf16)

    key_norm = normed(key_vectors, my_rstd[0], key_gain)
    query_norm = normed(query_vectors, my_rstd[1], query_gain)
    live = jnp.arange(block_pairs.shape[1], dtype=jnp.int32) < pair_counts[0]
    steps = block_pairs[0, :, 0] - block_pairs[0, :, 1]
    wanted = jnp.array(offsets, jnp.int32)
    flags = jnp.any(live[:, None] & (steps[:, None] == wanted[None, :]), axis=0)
    bias = jnp.pad(jnp.where(flags, 0.0, lowest), (0, TAIL - len(offsets)))
    allow = jnp.broadcast_to(bias[:, None], (TAIL, width)).astype(bf16)

    def cut(x, m, first, count):
        return lax.dynamic_slice_in_dim(x, (r ^ m) * width + first * HEAD, count * HEAD, axis=1)

    kv_cut = [
        [jnp.stack([cut(key_norm, m, *c), cut(value_vectors, m, *c)]) for m in range(group)]
        for c in plan.chunks
    ]
    qd_cut = [
        [
            jnp.concatenate(
                [cut(query_norm, m, *c), cut(output_grad, m, *c), allow[:, : c[1] * HEAD]]
            )
            for m in range(group)
        ]
        for c in plan.chunks
    ]

    def after(x, *earlier):
        return lax.optimization_barrier((x, earlier))[0]

    def swaps(xs):
        return [swap(x, m) for m, x in enumerate(xs)]

    half, last = group // 2, group - 1
    kv, qd = [], []
    arrived = None
    for c in range(len(plan.chunks)):
        mine = kv_cut[c] if arrived is None else after(kv_cut[c], arrived[half])
        arrived = swaps(mine)
        kv.append(arrived)
    for c in range(len(plan.chunks)):
        arrived = swaps(after(qd_cut[c], arrived[1 % group]))
        qd.append(arrived)
    halo = []
    for c in range(len(plan.chunks)):
        pack = jnp.stack(kv[c])
        if halo:
            pack = after(pack, qd[0][1 % group])
        halo.append([moved(pack, -by) for by in distances])
    kv = halo

    back = []
    oq_back = []
    for c, (first, count) in enumerate(plan.chunks):
        oq, kv_parts = attention(place, qd[c], kv[c], plan, first, count)
        sent = [moved(kv_parts[d], by) for d, by in enumerate(distances) if by]
        back.append((kv_parts[plan.home], sent))
        oq_back.append([swap(x, m) for m, x in enumerate(oq)])
    attended, query_norm_grad, query_inner = joined(
        place, oq_back, query_vectors, my_rstd[1:2], query_gain, plan
    )
    kv_back = []
    for own, sent in back:
        if kv_back:
            sent, kv_back[-1] = lax.optimization_barrier((sent, kv_back[-1]))
        total = []
        for m in range(group):
            x = own[m]
            for y in sent:
                x = x + y[m].astype(f32)
            total.append(swap(x.astype(bf16), m))
        kv_back.append(total)
    value_grad, key_norm_grad, key_inner = joined(
        place, kv_back, key_vectors, my_rstd[0:1], key_gain, plan
    )

    def finished(raw, rstd, gain, grad, inner):
        inner = summed(inner[:, 0])[:, None] / features
        rstd_col = rstd[0][:, None]
        unit = raw.astype(f32) * rstd_col
        return (rstd_col * (gain * grad.astype(f32) - unit * inner)).astype(bf16)

    query_grad = finished(query_vectors, my_rstd[1:2], query_gain, query_norm_grad, query_inner)
    key_grad = finished(key_vectors, my_rstd[0:1], key_gain, key_norm_grad, key_inner)
    return (attended, query_grad, key_grad, value_grad)


def solution(mesh):
    spans, head_groups = mesh.devices.shape
    plan = Plan(spans, DIM // HEAD // head_groups)
    blocks = Mesh(
        mesh.devices.reshape(spans // plan.group, plan.group, head_groups),
        ("block", "place", "head"),
    )
    ctx = ("block", "place")
    placed = (
        P(ctx, "head"),
        P(ctx, "head"),
        P(ctx, "head"),
        P(ctx, "head"),
        P("head"),
        P("head"),
        P(ctx, None, None),
        P(ctx),
    )
    return jax.shard_map(
        functools.partial(local, plan=plan),
        mesh=blocks,
        in_specs=placed,
        out_specs=(P(ctx, "head"),) * 4,
        check_vma=False,
    )
```

```python
import functools

import jax
import jax.numpy as jnp
import numpy as np
from jax import lax
from jax.experimental import pallas as pl
from jax.experimental.pallas import tpu as pltpu
from jax.sharding import Mesh
from jax.sharding import PartitionSpec as P

DIM = 5120
HEAD = 128
TAIL = 16
epsilon = 1e-06
lowest = -1e30
LOG2E = 1.4426950408889634
SCALE = HEAD ** (-0.5)
bf16 = jnp.bfloat16
f32 = jnp.float32
WIDE = pltpu.CompilerParams(vmem_limit_bytes=60 * 2**20)


def offset_list(levels):
    result = [0]
    for height in range(levels):
        result = result + [2**height, -(2**height)]
    return result


class Plan:
    def __init__(self, spans, heads_here):
        levels = spans.bit_length() - 2
        reach = 2 ** (levels - 1)
        whole = reach == 4 and heads_here % reach == 0 and spans % reach == 0
        self.group = reach if whole else 1
        self.offsets = sorted(offset_list(levels), reverse=True)
        self.distances = [-1, 0, 1] if self.group > 1 else sorted(self.offsets)
        self.home = self.distances.index(0)
        self.heads = heads_here // self.group
        self.chunks = chunks_of(self.heads)
        if self.group > 1:
            self.slots = [[self.group + s - o for o in self.offsets] for s in range(self.group)]
        else:
            self.slots = [[self.distances.index(-o) for o in self.offsets]]


def chunks_of(heads):
    first = (heads + 1) // 2
    return [(0, first), (first, heads - first)] if heads > 1 else [(0, heads)]


def busy(us):
    return pl.CostEstimate(flops=int(us * 1.1e9), bytes_accessed=int(us * 3.5e6), transcendentals=0)


def dot(a, b, ca, cb):
    return lax.dot_general(a, b, (((ca,), (cb,)), ((), ())), preferred_element_type=f32)


def attend(place, *refs, plan, first, heads):
    group, nd, noff = plan.group, len(plan.distances), len(plan.offsets)
    it = iter(refs)
    qd = [next(it) for _ in range(group)]
    kv = [[ref.at[m] for m in range(group)] for ref in [next(it) for _ in range(nd)]]
    out_oq = [next(it) for _ in range(group)]
    out_kv = [next(it) for _ in range(nd)]
    keys, vals, queries, grads, weights, scored, outs, dqs, allow = (next(it) for _ in range(9))
    r = place[0]

    def rows(slot):
        if isinstance(slot, int):
            return pl.ds(slot * HEAD, HEAD)
        return pl.ds(pl.multiple_of(slot * HEAD, HEAD), HEAD)

    def one_head(h, _):
        source = pl.ds(pl.multiple_of(h * HEAD, HEAD), HEAD)
        target = source
        for m in range(group):
            at = rows(m ^ r)
            queries[at, :] = qd[m][0:HEAD, source]
            grads[at, :] = qd[m][HEAD : 2 * HEAD, source]
            allow[m ^ r] = qd[m][2 * HEAD : 2 * HEAD + TAIL, source].astype(f32)
            for d in range(nd):
                at = rows(d * group + (m ^ r))
                keys[at, :] = kv[d][m][0, :, source]
                vals[at, :] = kv[d][m][1, :, source]

        def rows_of(j):
            return slice(j * HEAD, (j + 1) * HEAD)

        spans = range(group)
        q = [queries[rows(s), :] for s in spans]
        g = [grads[rows(s), :] for s in spans]
        k = [jnp.concatenate([keys[rows(x), :] for x in plan.slots[s]], axis=0) for s in spans]
        v = [jnp.concatenate([vals[rows(x), :] for x in plan.slots[s]], axis=0) for s in spans]
        raw = [dot(q[s], k[s], 1, 1) for s in spans]
        dp = [dot(g[s], v[s], 1, 1) for s in spans]
        p = []
        for s in spans:
            bias = jnp.concatenate([allow[s, j : j + 1, :] for j in range(noff)], axis=1)
            scores = raw[s] * (SCALE * LOG2E) + bias
            e = jnp.exp2(scores - jnp.max(scores, axis=1, keepdims=True))
            p.append(e * (1.0 / jnp.sum(e, axis=1, keepdims=True)))
        low = [x.astype(bf16) for x in p]
        o = [dot(low[s], v[s], 1, 0).astype(bf16) for s in spans]
        ds = []
        for s in spans:
            delta = jnp.sum(g[s].astype(f32) * o[s].astype(f32), axis=1, keepdims=True)
            ds.append((p[s] * SCALE * (dp[s] - delta)).astype(bf16))
        for s in spans:
            outs[rows(s), :] = o[s]
            dqs[rows(s), :] = dot(ds[s], k[s], 1, 0).astype(bf16)

        for m in range(group):
            out_oq[m][0, :, target] = outs[rows(m ^ r), :]
            out_oq[m][1, :, target] = dqs[rows(m ^ r), :]

        for d in range(nd):
            for s in range(group):
                users = [
                    (t, j)
                    for t in range(group)
                    for j in range(noff)
                    if plan.slots[t][j] == d * group + s
                ]

                def stacked(values):
                    return jnp.concatenate([values[t][:, rows_of(j)] for t, j in users], axis=0)

                qs = jnp.concatenate([q[t] for t, _ in users], axis=0)
                gs = jnp.concatenate([g[t] for t, _ in users], axis=0)
                out_kv[d][s ^ r, 1, :, target] = dot(stacked(ds), qs, 0, 0).astype(out_kv[d].dtype)
                out_kv[d][s ^ r, 0, :, target] = dot(stacked(low), gs, 0, 0).astype(out_kv[d].dtype)
        return 0

    lax.fori_loop(0, heads, one_head, 0)


def attention(place, qd, kv, plan, first, heads):
    width = heads * HEAD
    group, nd, noff = plan.group, len(plan.distances), len(plan.offsets)
    ng = nd * group
    whole = pl.BlockSpec(memory_space=pltpu.VMEM)
    args = [place, *qd, *kv]
    outs = [jax.ShapeDtypeStruct((2, HEAD, width), bf16)] * group + [
        jax.ShapeDtypeStruct((group, 2, HEAD, width), f32 if by == 0 else bf16)
        for by in plan.distances
    ]
    result = pl.pallas_call(
        functools.partial(attend, plan=plan, first=first, heads=heads),
        grid_spec=pltpu.PrefetchScalarGridSpec(
            num_scalar_prefetch=1,
            grid=(),
            in_specs=[whole] * (len(args) - 1),
            out_specs=[whole] * (group + nd),
            scratch_shapes=[pltpu.VMEM((ng * HEAD, HEAD), bf16)] * 2
            + [pltpu.VMEM((group * HEAD, HEAD), bf16)] * 2
            + [pltpu.VMEM((group * HEAD, noff * HEAD), bf16)] * 2
            + [pltpu.VMEM((group * HEAD, HEAD), bf16)] * 2
            + [pltpu.VMEM((group, TAIL, HEAD), f32)],
        ),
        out_shape=outs,
        compiler_params=pltpu.CompilerParams(vmem_limit_bytes=36 * 2**20),
        cost_estimate=busy(10 * heads),
        name="attend",
    )(*args)
    return result[:group], result[group:]


def join(place, *refs, plan):
    group = plan.group
    count = len(plan.chunks) * group
    parts = refs[:count]
    raw_ref, rstd_ref, gain_ref, plain, normed, inner = refs[count:]
    r = place[0]
    column = jnp.transpose(jnp.broadcast_to(rstd_ref[...], (HEAD, HEAD)))[:, 0:1]
    width = plan.heads * HEAD
    total = jnp.zeros((HEAD, HEAD), f32)
    for c, (first, heads) in enumerate(plan.chunks):
        for m in range(group):
            base = (m ^ r) * width + first * HEAD
            part = parts[c * group + m]
            for h in range(heads):
                at = pl.ds(pl.multiple_of(base + h * HEAD, HEAD), HEAD)
                here = slice(h * HEAD, (h + 1) * HEAD)
                plain[:, at] = part[0, :, here]
                low = part[1, :, here]
                normed[:, at] = low
                total += low.astype(f32) * gain_ref[:, at] * raw_ref[:, at].astype(f32)
    inner[...] = jnp.broadcast_to(
        jnp.sum(total, axis=1, keepdims=True) * column, (HEAD, HEAD)
    )


def joined(place, parts, raw, rstd, gain, plan):
    shape = raw.shape
    flat = [x for chunk in parts for x in chunk]
    whole = pl.BlockSpec(memory_space=pltpu.VMEM)
    return pl.pallas_call(
        functools.partial(join, plan=plan),
        grid_spec=pltpu.PrefetchScalarGridSpec(
            num_scalar_prefetch=1,
            grid=(),
            in_specs=[whole] * (len(flat) + 3),
            out_specs=[whole] * 3,
        ),
        out_shape=[
            jax.ShapeDtypeStruct(shape, bf16),
            jax.ShapeDtypeStruct(shape, bf16),
            jax.ShapeDtypeStruct((HEAD, HEAD), f32),
        ],
        compiler_params=pltpu.CompilerParams(vmem_limit_bytes=24 * 2**20),
        cost_estimate=busy(2),
        name="join",
    )(place, *flat, raw, rstd, gain)


def local(
    query_vectors,
    key_vectors,
    value_vectors,
    output_grad,
    query_gain,
    key_gain,
    block_pairs,
    pair_counts,
    *,
    plan,
):
    row_count, col_count = query_vectors.shape
    group, offsets, distances = plan.group, plan.offsets, plan.distances
    features = col_count * lax.axis_size("head")
    width = col_count // group
    blocks = lax.axis_size("block")
    r = lax.axis_index("place")
    place = jnp.reshape(r, (1,)).astype(jnp.int32)

    def swap(x, m):
        return lax.ppermute(x, "place", [(i, i ^ m) for i in range(group)]) if m else x

    def moved(x, by):
        if by == 0:
            return x
        return lax.ppermute(
            x, "block", [(i, i + by) for i in range(blocks) if 0 <= i + by < blocks]
        )

    def summed(x):
        step, count = 1, lax.axis_size("head")
        while step < count:
            x = x + lax.ppermute(x, "head", [(i, i ^ step) for i in range(count)])
            step *= 2
        return x

    query_gain = query_gain[None, :]
    key_gain = key_gain[None, :]

    def chunk(x, m):
        return lax.dynamic_slice_in_dim(x, (r ^ m) * width, width, axis=1)

    squares = summed(
        jnp.stack([jnp.sum(jnp.square(x.astype(f32)), axis=1) for x in (key_vectors, query_vectors)])
    )
    my_rstd = lax.rsqrt(squares / features + epsilon)

    def normed(x, rstd, gain):
        return (x.astype(f32) * rstd[:, None] * gain).astype(bf16)

    key_norm = normed(key_vectors, my_rstd[0], key_gain)
    query_norm = normed(query_vectors, my_rstd[1], query_gain)
    live = jnp.arange(block_pairs.shape[1], dtype=jnp.int32) < pair_counts[0]
    steps = block_pairs[0, :, 0] - block_pairs[0, :, 1]
    wanted = jnp.array(offsets, jnp.int32)
    flags = jnp.any(live[:, None] & (steps[:, None] == wanted[None, :]), axis=0)
    bias = jnp.pad(jnp.where(flags, 0.0, lowest), (0, TAIL - len(offsets)))
    allow = jnp.broadcast_to(bias[:, None], (TAIL, width)).astype(bf16)

    def cut(x, m, first, count):
        return lax.dynamic_slice_in_dim(x, (r ^ m) * width + first * HEAD, count * HEAD, axis=1)

    kv_cut = [
        [jnp.stack([cut(key_norm, m, *c), cut(value_vectors, m, *c)]) for m in range(group)]
        for c in plan.chunks
    ]
    qd_cut = [
        [
            jnp.concatenate(
                [cut(query_norm, m, *c), cut(output_grad, m, *c), allow[:, : c[1] * HEAD]]
            )
            for m in range(group)
        ]
        for c in plan.chunks
    ]

    def after(x, *earlier):
        return lax.optimization_barrier((x, earlier))[0]

    def swaps(xs):
        return [swap(x, m) for m, x in enumerate(xs)]

    half, last = group // 2, group - 1
    kv, qd = [], []
    arrived = None
    for c in range(len(plan.chunks)):
        mine = kv_cut[c] if arrived is None else after(kv_cut[c], arrived[half])
        arrived = swaps(mine)
        kv.append(arrived)
    for c in range(len(plan.chunks)):
        arrived = swaps(after(qd_cut[c], arrived[1 % group]))
        qd.append(arrived)
    halo = []
    for c in range(len(plan.chunks)):
        pack = jnp.stack(kv[c])
        if halo:
            pack = after(pack, qd[0][1 % group])
        halo.append([moved(pack, -by) for by in distances])
    kv = halo

    back = []
    oq_back = []
    for c, (first, count) in enumerate(plan.chunks):
        oq, kv_parts = attention(place, qd[c], kv[c], plan, first, count)
        sent = [moved(kv_parts[d], by) for d, by in enumerate(distances) if by]
        back.append((kv_parts[plan.home], sent))
        oq_back.append([swap(x, m) for m, x in enumerate(oq)])
    attended, query_norm_grad, query_inner = joined(
        place, oq_back, query_vectors, my_rstd[1:2], query_gain, plan
    )
    kv_back = []
    for own, sent in back:
        if kv_back:
            sent, kv_back[-1][half] = lax.optimization_barrier((sent, kv_back[-1][half]))
        total = []
        for m in range(group):
            x = own[m]
            for y in sent:
                x = x + y[m].astype(f32)
            total.append(swap(x.astype(bf16), m))
        kv_back.append(total)
    value_grad, key_norm_grad, key_inner = joined(
        place, kv_back, key_vectors, my_rstd[0:1], key_gain, plan
    )

    def finished(raw, rstd, gain, grad, inner):
        inner = summed(inner[:, 0])[:, None] / features
        rstd_col = rstd[0][:, None]
        unit = raw.astype(f32) * rstd_col
        return (rstd_col * (gain * grad.astype(f32) - unit * inner)).astype(bf16)

    query_grad = finished(query_vectors, my_rstd[1:2], query_gain, query_norm_grad, query_inner)
    key_grad = finished(key_vectors, my_rstd[0:1], key_gain, key_norm_grad, key_inner)
    return (attended, query_grad, key_grad, value_grad)


def solution(mesh):
    spans, head_groups = mesh.devices.shape
    plan = Plan(spans, DIM // HEAD // head_groups)
    blocks = Mesh(
        mesh.devices.reshape(spans // plan.group, plan.group, head_groups),
        ("block", "place", "head"),
    )
    ctx = ("block", "place")
    placed = (
        P(ctx, "head"),
        P(ctx, "head"),
        P(ctx, "head"),
        P(ctx, "head"),
        P("head"),
        P("head"),
        P(ctx, None, None),
        P(ctx),
    )
    return jax.shard_map(
        functools.partial(local, plan=plan),
        mesh=blocks,
        in_specs=placed,
        out_specs=(P(ctx, "head"),) * 4,
        check_vma=False,
    )
```
